256 devices in a mesh: gx: 32 (over z, y), gy: 8 (over x, core).
Axes of the slice: x: 4, y: 4, z: 8, core: 2. Of those that a mesh axis runs over, the one named last changes fastest.
Arguments:
- density: float32 [256, 512, 256], P('gx', 'gy'), may hold values from 0.6 to 1.6
- momentum: float32 [3, 256, 512, 256], P(None, 'gx', 'gy'), may hold values from -0.6 to 2.1
- energy: float32 [256, 512, 256], P('gx', 'gy'), may hold values from 2 to 4
- snapshots: bfloat16 [63, 3, 64, 8192], P(None, None, 'gx', 'gy'), may hold values from -3.9 to 9.9
Outputs:
- new_density: float32 [256, 512, 256], P('gx', 'gy')
- new_momentum: float32 [3, 256, 512, 256], P(None, 'gx', 'gy')
- new_energy: float32 [256, 512, 256], P('gx', 'gy')
- pod_factor: float32 [64, 64], replicated
- pod_modes: float32 [64, 3, 64, 8192], P(None, None, 'gx', 'gy')
The draws below stay inside these ranges and needn't reach their ends.
All inputs are finite; a program needn't handle non-finite values.
Results may differ from the reference program's by a relative error of at most 0.00035.
Values sent between devices are 32-bit elements; how exact they have to be, the bound alone decides.
A program may use at most 128 MiB of HBM per device.

```python
import jax
import jax.numpy as jnp
from jax import lax

CX = 8
CY = 64
NZ = 256
SNAPS = 63
NX = 256
NY = 512
ROWS = 1572864


def profile(position, count):
    centered = (2.0 * position + 1.0) / count - 1.0
    return 1.5 * (1.0 - centered * centered)


def draw_momentum(key, part):
    noise_key = jax.random.fold_in(key, 11)
    shape = (3, NX, NY, NZ)
    noise = jnp.clip(0.3 * jax.random.normal(noise_key, shape, jnp.float32), -0.6, 0.6)
    heights = jnp.arange(NZ).astype(jnp.float32)
    streamwise = noise[0] + profile(heights, NZ)[None, None, :]
    return jnp.concatenate([streamwise[None], noise[1:]], axis=0)


def draw_snapshots(key, part):
    amp_key = jax.random.fold_in(key, 21)
    noise_key = jax.random.fold_in(key, 22)
    xscale_key = jax.random.fold_in(key, 23)
    yscale_key = jax.random.fold_in(key, 24)
    shape = (SNAPS, 3, NX // 4, NY // 4 * (NZ // 4))
    amplitude = jax.random.uniform(amp_key, (SNAPS,), jnp.float32, 0.6, 1.4)
    noise = jnp.clip(jax.random.normal(noise_key, shape, jnp.float32), -3.0, 3.0)
    streamwise_pos = jnp.arange(NX // 4)
    ramp = 0.15 * (1.0 + 2.0 * streamwise_pos.astype(jnp.float32) / max(NX // 4 - 1, 1))
    flat_pos = jnp.arange(NY // 4 * (NZ // 4))
    coarse_z = (flat_pos % (NZ // 4)).astype(jnp.float32)
    spanwise_pos = flat_pos // (NZ // 4)
    xfactors = jnp.exp(jax.random.uniform(xscale_key, (NX // 4,), jnp.float32, -0.35, 0.35))
    yfactors = jnp.exp(jax.random.uniform(yscale_key, (NY // 4,), jnp.float32, -0.7, 0.7))
    xscale = xfactors[streamwise_pos // (CX // 4)]
    yscale = yfactors[spanwise_pos // (CY // 4)]
    mean_part = profile(4.0 * coarse_z + 1.5, NZ)
    component = (jnp.arange(3) == 0).astype(jnp.float32)
    values = amplitude[:, None, None, None] * component[None, :, None, None] * mean_part[None, None, None, :] + ramp[None, None, :, None] * noise
    values = values * xscale[None, None, :, None] * yscale[None, None, None, :]
    return values.astype(jnp.bfloat16)


def levels(key, shape, shards, low, largest):
    def one(axis_at, parts):
        steps = jax.random.uniform(jax.random.fold_in(jax.random.fold_in(key, 6), axis_at), (parts,), jnp.float32, low / len(shards), largest / len(shards))
        return jnp.repeat(jnp.exp(steps), shape[axis_at] // parts).reshape((-1,) + (1,) * (len(shape) - axis_at - 1))

    level = one(*shards[0])
    for cut in shards[1:]:
        level = level * one(*cut)
    return level


def setup_inputs(seed: int = 0) -> dict:
    arg_keys = jax.random.split(jax.random.key(seed), 5)
    density = jnp.clip(0.6 + 1.0 * jax.random.uniform(arg_keys[0], (NX, NY, NZ), jnp.float32) ** levels(arg_keys[0], (NX, NY, NZ), ((0, 32), (1, 8)), -0.2, 0.2), 0.6, 1.6)
    momentum = draw_momentum(jax.random.fold_in(arg_keys[4], 71), 0)
    energy = jnp.clip(2.0 + 2.0 * jax.random.uniform(arg_keys[2], (NX, NY, NZ), jnp.float32) ** levels(arg_keys[2], (NX, NY, NZ), ((0, 32), (1, 8)), -0.2, 0.2), 2.0, 4.0)
    snapshots = draw_snapshots(jax.random.fold_in(arg_keys[4], 71), 0)
    return {"density": density, "momentum": momentum, "energy": energy, "snapshots": snapshots}


time_step = 0.08
shear_friction_coefficient = 1.5
heat_conduction_coefficient = 1.5

def sheet_curvature_operator(field):
    return field[..., 2:, 1:-1, :] + field[..., :-2, 1:-1, :] + field[..., 1:-1, 2:, :] + field[..., 1:-1, :-2, :] - 4.0 * field[..., 1:-1, 1:-1, :]

def boundary_couple(center, copied):
    if copied:
        upper_cell = jnp.concatenate([center[..., 1:], center[..., -1:]], axis=-1)
        lower_cell = jnp.concatenate([center[..., :1], center[..., :-1]], axis=-1)
    else:
        zeros_row = jnp.zeros_like(center[..., :1])
        upper_cell = jnp.concatenate([center[..., 1:], zeros_row], axis=-1)
        lower_cell = jnp.concatenate([zeros_row, center[..., :-1]], axis=-1)
    return (upper_cell, lower_cell)

def tendency(padded):
    mass_density_grid = padded[0]
    momenta = padded[1:4]
    total_energy_grid = padded[4]
    velocity = momenta / mass_density_grid
    heat_condition_fields = total_energy_grid / mass_density_grid
    vel_center = velocity[:, 1:-1, 1:-1, :]
    vel_upper, vel_lower = boundary_couple(vel_center, False)
    velocity_second_derivative_sum = sheet_curvature_operator(velocity) + vel_upper + vel_lower - 2.0 * vel_center
    central_heat_value = heat_condition_fields[1:-1, 1:-1, :]
    upper_neighbour_heat, lower_neighbour_heat = boundary_couple(central_heat_value, True)
    heat_curvature_sum = sheet_curvature_operator(heat_condition_fields) + upper_neighbour_heat + lower_neighbour_heat - 2.0 * central_heat_value
    normal_upper, normal_lower = boundary_couple(momenta[2][1:-1, 1:-1, :], False)
    flux_spread_rate = 0.5 * (momenta[0][2:, 1:-1, :] - momenta[0][:-2, 1:-1, :] + (momenta[1][1:-1, 2:, :] - momenta[1][1:-1, :-2, :]) + (normal_upper - normal_lower))
    return jnp.concatenate([(-flux_spread_rate)[None], shear_friction_coefficient * velocity_second_derivative_sum, (heat_conduction_coefficient * heat_curvature_sum)[None]], axis=0)

def periodic(state):
    return jnp.pad(state, ((0, 0), (1, 1), (1, 1), (0, 0)), mode='wrap')

def reference(density, momentum, energy, snapshots):
    state = jnp.concatenate([density[None], momentum, energy[None]], axis=0)
    sectioned = state + time_step * tendency(periodic(state))
    updated = 0.5 * state + 0.5 * (sectioned + time_step * tendency(periodic(sectioned)))
    velocity = updated[1:4] / updated[0]
    coarse = velocity.reshape(3, NX // 4, 4, NY // 4, 4, NZ // 4, 4).mean(axis=(2, 4, 6))
    coarse = coarse.reshape(1, -1)
    stored = snapshots.astype(jnp.float32).reshape(SNAPS, -1)
    columns = jnp.concatenate([stored, coarse], axis=0)
    gram = jnp.dot(columns.astype(jnp.float32), columns.T.astype(jnp.float32), precision=lax.Precision.HIGHEST, preferred_element_type=jnp.float32) / ROWS
    pod_factor = jnp.linalg.cholesky(gram).T
    modes = lax.linalg.triangular_solve(pod_factor, columns, left_side=True, lower=False, transpose_a=True)
    pod_modes = modes.reshape(SNAPS + 1, 3, NX // 4, NY // 4 * (NZ // 4))
    return (updated[0], updated[1:4], updated[4], pod_factor, pod_modes)
```

```python
import functools

import jax
import jax.numpy as jnp
from jax import lax
from jax.experimental import pallas as pl
from jax.experimental.pallas import tpu as pltpu
from jax.sharding import PartitionSpec as P

f32 = jnp.float32
bf16 = jnp.bfloat16
MESH = pl.DeviceIdType.MESH

time_step = 0.08
shear_friction_coefficient = 1.5
heat_conduction_coefficient = 1.5

X, Y, Z = 8, 64, 256
XP, YP = 12, 80
STEP_X = 2 * YP
SNAPS = 63
BLOCKS = 48
CHUNK = 32


def flat(ref):
    rows = 1
    for size in ref.shape[:-1]:
        rows *= size
    return ref.reshape(rows, 128)


def split3(value):
    high = value.astype(bf16)
    rest = value - high.astype(f32)
    middle = rest.astype(bf16)
    low = (rest - middle.astype(f32)).astype(bf16)
    return high, middle, low


def z_pair(pair, copied):
    low, high = pair
    lane = lax.broadcasted_iota(jnp.int32, low.shape, 1)
    last, first = lane == 127, lane == 0
    low_up, high_up = pltpu.roll(low, 127, 1), pltpu.roll(high, 127, 1)
    low_down, high_down = pltpu.roll(low, 1, 1), pltpu.roll(high, 1, 1)
    above, below = (high, low) if copied else (0.0, 0.0)
    up = (jnp.where(last, high_up, low_up), jnp.where(last, above, high_up))
    down = (jnp.where(first, below, low_down), jnp.where(first, low_down, high_down))
    return up, down


def primitives(state):
    inverse = 1.0 / state[0]
    return [state[1 + field] * inverse for field in range(4)]


def change(center, x_up, x_down, y_up, y_down, mx_up, mx_down, my_up, my_down, mz):
    up, down = z_pair(mz, False)
    result = [
        [
            (-0.5 * time_step) * ((mx_up[t] - mx_down[t]) + (my_up[t] - my_down[t]) + (up[t] - down[t]))
            for t in range(2)
        ]
    ]
    for field in range(4):
        rate = heat_conduction_coefficient if field == 3 else shear_friction_coefficient
        up, down = z_pair(center[field], field == 3)
        result.append(
            [
                (time_step * rate)
                * (
                    (x_up[field][t] + x_down[field][t])
                    + (y_up[field][t] + y_down[field][t])
                    + (up[t] + down[t])
                    - 6.0 * center[field][t]
                )
                for t in range(2)
            ]
        )
    return result


def change_rows(prim, state, x, row, count):
    def v(dx, dy):
        return [[prim[f, x + dx, t, pl.ds(row + dy, count), :] for t in range(2)] for f in range(4)]

    def s(field, dx, dy):
        return [state[field, x + dx, t, pl.ds(row + dy, count), :] for t in range(2)]

    return change(
        v(0, 0), v(1, 0), v(-1, 0), v(0, 1), v(0, -1),
        s(1, 1, 0), s(1, -1, 0), s(2, 0, 1), s(2, 0, -1), s(3, 0, 0),
    )


def primitive_layer(state, prim, x):
    for row in range(8, 8 + Y, CHUNK):
        for t in range(2):
            values = primitives([state[f, x, t, pl.ds(row, CHUNK), :] for f in range(5)])
            for f in range(4):
                prim[f, x, t, pl.ds(row, CHUNK), :] = values[f]


def first_layer(state, prim, state2, prim2, x):
    for row in range(8, 8 + Y, CHUNK):
        delta = change_rows(prim, state, x, row, CHUNK)
        for t in range(2):
            new = [state[f, x, t, pl.ds(row, CHUNK), :] + delta[f][t] for f in range(5)]
            values = primitives(new)
            for f in range(5):
                state2[f, x, t, pl.ds(row, CHUNK), :] = new[f]
            for f in range(4):
                prim2[f, x, t, pl.ds(row, CHUNK), :] = values[f]


def second_layer(state, state2, prim2, updated, sums, x):
    for row in range(8, 8 + Y, CHUNK):
        delta = change_rows(prim2, state2, x, row, CHUNK)
        for t in range(2):
            new = [
                0.5 * state[f, x, t, pl.ds(row, CHUNK), :]
                + 0.5 * (state2[f, x, t, pl.ds(row, CHUNK), :] + delta[f][t])
                for f in range(5)
            ]
            inverse = 1.0 / new[0]
            for f in range(5):
                updated[f, x - 2, t, pl.ds(row - 8, CHUNK), :] = new[f]
            for c in range(3):
                sums[c, (x - 2) // 4, t, pl.ds(row - 8, CHUNK), :] += new[1 + c] * inverse


def sheet(field, tile, row, dx=0):
    return pl.ds(((field * XP + 2 + dx) * 2 + tile) * YP + row, X, stride=STEP_X)


def place_rows(state, prim, y_in, side):
    row = 7 if side == 0 else 72
    flat_state, flat_prim = flat(state), flat(prim)
    for t in range(2):
        near = [y_in[side, f, 0, t] for f in range(5)]
        values = primitives(near)
        for f in range(4):
            flat_prim[sheet(f, t, row), :] = values[f]
        for f in (1, 2):
            flat_state[sheet(f, t, row), :] = near[f]


def place_corner(state, prim, corner_in, side_x, side_y):
    x = 1 if side_x == 0 else 10
    row = 7 if side_y == 0 else 72
    for t in range(2):
        values = corner_in[side_x, side_y, t]
        inverse = 1.0 / values[0:1]
        for f in range(4):
            prim[f, x, t, pl.ds(row, 1), :] = values[1 + f : 2 + f] * inverse
        for f in (1, 2):
            state[f, x, t, pl.ds(row, 1), :] = values[f : f + 1]


def edge_rows(state, prim, state2, prim2, y_in, side):
    row, own = (7, 8) if side == 0 else (72, 71)
    flat_state, flat_prim = flat(state), flat(prim)
    flat_state2, flat_prim2 = flat(state2), flat(prim2)

    def v(at, dx):
        return [[flat_prim[sheet(f, t, at, dx), :] for t in range(2)] for f in range(4)]

    def s(field, at, dx):
        return [flat_state[sheet(field, t, at, dx), :] for t in range(2)]

    near = [[y_in[side, f, 0, t] for f in range(5)] for t in range(2)]
    far = [primitives([y_in[side, f, 1, t] for f in range(5)]) for t in range(2)]
    far = [[far[t][f] for t in range(2)] for f in range(4)]
    far_my = [y_in[side, 2, 1, t] for t in range(2)]
    inner, inner_my = v(own, 0), s(2, own, 0)
    y_up, y_down, my_up, my_down = (
        (inner, far, inner_my, far_my) if side == 0 else (far, inner, far_my, inner_my)
    )
    delta = change(
        v(row, 0), v(row, 1), v(row, -1), y_up, y_down,
        s(1, row, 1), s(1, row, -1), my_up, my_down, [near[t][3] for t in range(2)],
    )
    for t in range(2):
        new = [near[t][f] + delta[f][t] for f in range(5)]
        values = primitives(new)
        for f in range(4):
            flat_prim2[sheet(f, t, row), :] = values[f]
        flat_state2[sheet(2, t, row), :] = new[2]


def eliminate(rows):
    sub = lax.broadcasted_iota(jnp.int32, (8, 128), 0)
    for k in range(SNAPS):
        block, at = divmod(k, 8)
        row = jnp.broadcast_to(rows[block][at : at + 1, :], (8, 128))
        pivot = jnp.broadcast_to(row[:, k : k + 1], (8, 128))
        scaled = row * (1.0 / pivot)
        for b in range(block, 8):
            column = jnp.broadcast_to(rows[b][:, k : k + 1], (8, 128))
            if b == block:
                column = jnp.where(sub > at, column, 0.0)
            rows[b] = rows[b] - column * scaled
    return rows


def kernel(
    rows_all, sizes,
    density, momentum, energy, snapshots,
    out_density, out_momentum, out_energy, out_factor, out_modes,
    state, prim, state2, prim2, updated, sums,
    y_out, y_in, corner_out, corner_in,
    snap_in, snap_f, snap_b, modes, factor_v, coarse,
    gram, gram_part, gram_z, gram_y, gram_all, gram_sums,
    dot_gy, dot_z, dot_y, dot_sums,
    load_sem, store_sem,
    x_send, x_recv, y_send, y_recv, corner_send, corner_recv,
    gram_send, gram_recv, dot_send, dot_recv,
):
    n_gx, n_gy, n_y = sizes
    n_z = n_gx // n_y
    gx, gy = lax.axis_index("gx"), lax.axis_index("gy")
    iz, iy = lax.div(gx, n_y), lax.rem(gx, n_y)

    def moved(dx, dy):
        return {"gx": lax.rem(gx + dx + n_gx, n_gx), "gy": lax.rem(gy + dy + n_gy, n_gy)}

    def on_gy(i):
        return {"gx": gx, "gy": i}

    def on_z(i):
        return {"gx": i * n_y + iy, "gy": gy}

    def on_y(i):
        return {"gx": iz * n_y + i, "gy": gy}

    loads = []
    for t in range(2):
        lanes, rows = pl.ds(128 * t, 128), pl.ds(8, Y)
        loads += [
            pltpu.make_async_copy(density.at[:, :, lanes], state.at[0, pl.ds(2, X), t, rows, :], load_sem.at[3 * t]),
            pltpu.make_async_copy(
                momentum.at[:, :, :, lanes], state.at[pl.ds(1, 3), pl.ds(2, X), t, rows, :], load_sem.at[3 * t + 1]
            ),
            pltpu.make_async_copy(energy.at[:, :, lanes], state.at[4, pl.ds(2, X), t, rows, :], load_sem.at[3 * t + 2]),
        ]
    load_snapshots = pltpu.make_async_copy(snapshots, snap_in, load_sem.at[6])
    for copy in loads:
        copy.start()
    load_snapshots.start()

    barrier = pltpu.get_barrier_semaphore()
    greeted = [moved(dx, dy) for dx in (-1, 1) for dy in (-1, 0, 1)]
    greeted += [on_gy(lax.rem(gy + d, n_gy)) for d in range(1, n_gy)]
    greeted += [on_z(lax.rem(iz + d, n_z)) for d in range(1, n_z)]
    greeted += [on_y(lax.rem(iy + d, n_y)) for d in range(1, n_y)]
    for device in greeted:
        pl.semaphore_signal(barrier, inc=1, device_id=device, device_id_type=MESH)
    pl.semaphore_wait(barrier, len(greeted))

    def remote(source, target, send_sem, recv_sem, device):
        return pltpu.make_async_remote_copy(
            src_ref=source, dst_ref=target, send_sem=send_sem, recv_sem=recv_sem, device_id=device, device_id_type=MESH
        )

    def x_copies(layer):
        copies = []
        for side in range(2):
            source, target = (X - 1 - layer, 1 - layer) if side == 0 else (layer, 10 + layer)
            device = moved(1, 0) if side == 0 else moved(-1, 0)
            for t in range(2):
                lanes, rows = pl.ds(128 * t, 128), pl.ds(8, Y)
                at = ((layer * 2 + side) * 2 + t) * 3
                copies += [
                    remote(
                        density.at[source, :, lanes], state.at[0, target, t, rows, :],
                        x_send.at[at], x_recv.at[at], device,
                    ),
                    remote(
                        momentum.at[:, source, :, lanes], state.at[pl.ds(1, 3), target, t, rows, :],
                        x_send.at[at + 1], x_recv.at[at + 1], device,
                    ),
                    remote(
                        energy.at[source, :, lanes], state.at[4, target, t, rows, :],
                        x_send.at[at + 2], x_recv.at[at + 2], device,
                    ),
                ]
        return copies

    near_copies, far_copies = x_copies(0), x_copies(1)
    for copy in near_copies:
        copy.start()

    for copy in loads:
        copy.wait()
    flat_state = flat(state)
    for side in range(2):
        for f in range(5):
            for far in range(2):
                y = Y - 1 - far if side == 0 else far
                for t in range(2):
                    y_out[side, f, far, t] = flat_state[sheet(f, t, 8 + y), :]
    y_copies = [
        remote(y_out.at[side], y_in.at[side], y_send.at[side], y_recv.at[side], moved(0, 1 - 2 * side))
        for side in range(2)
    ]
    for copy in y_copies:
        copy.start()
    corner_out[...] = jnp.zeros_like(corner_out)
    corner_copies = []
    for side_x in range(2):
        for side_y in range(2):
            x, y = (X - 1) * (1 - side_x), (Y - 1) * (1 - side_y)
            for t in range(2):
                start = ((2 + x) * 2 + t) * YP + 8 + y
                corner_out[side_x, side_y, t, 0:5] = flat_state[pl.ds(start, 5, stride=XP * STEP_X), :]
            at = side_x * 2 + side_y
            corner_copies.append(
                remote(
                    corner_out.at[side_x, side_y], corner_in.at[side_x, side_y],
                    corner_send.at[at], corner_recv.at[at], moved(1 - 2 * side_x, 1 - 2 * side_y),
                )
            )
    for copy in corner_copies:
        copy.start()

    load_snapshots.wait()
    for c in range(3):
        snap_f[0:SNAPS, c] = snap_in[:, c].astype(f32)
    snap_f[SNAPS] = jnp.zeros((3, 16, 128), f32)
    flat_snap, flat_modes = flat(snap_f), flat(modes)

    def gram_step(i, total):
        pair = jnp.concatenate([flat_snap[pl.ds(2 * i + half, 64, stride=BLOCKS), :] for half in range(2)], axis=1)
        pair = pair.astype(bf16)
        snap_b[i] = pair
        return total + lax.dot_general(pair, pair, (((1,), (1,)), ((), ())), preferred_element_type=f32)

    local = lax.fori_loop(0, BLOCKS // 2, gram_step, jnp.zeros((64, 64), f32))
    local = jnp.concatenate([local, jnp.zeros((64, 64), f32)], axis=1)
    for b in range(8):
        gram[b] = local[8 * b : 8 * b + 8]

    def exchange(sources, target, me, count, device_of, send, recv, first):
        copies = []
        for d in range(1, count):
            peer = lax.rem(me + d, count)
            copies.append(
                remote(sources(peer), target.at[me], send.at[first + d], recv.at[first + d], device_of(peer))
            )
        for copy in copies:
            copy.start()
        return copies

    def total(ref, count):
        value = ref[0]
        for i in range(1, count):
            value = value + ref[i]
        return value

    copies = exchange(lambda peer: gram.at[peer], gram_part, gy, n_gy, on_gy, gram_send, gram_recv, 0)
    gram_part[gy] = gram[gy]

    def loop(start, stop, step):
        lax.fori_loop(start, stop, lambda x, _: (step(x), 0)[1], 0)

    loop(2, 2 + X, lambda x: primitive_layer(state, prim, x))
    for copy in copies:
        copy.wait()
    gram_sums[0] = total(gram_part, n_gy)
    copies = exchange(lambda peer: gram_sums.at[0], gram_z, iz, n_z, on_z, gram_send, gram_recv, 8)
    gram_z[iz] = gram_sums[0]
    for copy in y_copies:
        copy.wait()
    for side in range(2):
        place_rows(state, prim, y_in, side)
    loop(3, 1 + X, lambda x: first_layer(state, prim, state2, prim2, x))
    for copy in copies:
        copy.wait()
    gram_sums[1] = total(gram_z, n_z)
    copies = exchange(lambda peer: gram_sums.at[1], gram_y, iy, n_y, on_y, gram_send, gram_recv, 16)
    gram_y[iy] = gram_sums[1]
    for copy in far_copies:
        copy.start()
    for copy in copies:
        copy.wait()
    gram_sums[2] = total(gram_y, n_y)
    copies = exchange(lambda peer: gram_sums.at[2], gram_all, gy, n_gy, on_gy, gram_send, gram_recv, 24)
    gram_all[gy] = gram_sums[2]

    sums[...] = jnp.zeros_like(sums)
    for copy in near_copies + corner_copies:
        copy.wait()
    loop(0, 2, lambda i: primitive_layer(state, prim, 1 + 9 * i))
    for side_x in range(2):
        for side_y in range(2):
            place_corner(state, prim, corner_in, side_x, side_y)
    loop(0, 2, lambda i: first_layer(state, prim, state2, prim2, 2 + 7 * i))
    for side in range(2):
        edge_rows(state, prim, state2, prim2, y_in, side)
    for copy in copies:
        copy.wait()

    lane = lax.broadcasted_iota(jnp.int32, (8, 128), 1)
    sub = lax.broadcasted_iota(jnp.int32, (8, 128), 0)
    blocks = []
    for b in range(8):
        row = sub + 8 * b
        known = (row < SNAPS) & (lane < SNAPS)
        unit = ((lane == row) & (row == SNAPS)) | (lane == row + 64)
        blocks.append(jnp.where(known, gram_all[b] / rows_all, jnp.where(unit, 1.0, 0.0)))
    blocks = eliminate(blocks)
    lower = []
    for b in range(8):
        row = sub + 8 * b
        diagonal = jnp.sum(jnp.where(lane == row, blocks[b], 0.0), axis=1, keepdims=True)
        scaled = blocks[b] * (1.0 / jnp.sqrt(diagonal))
        factor_v[b] = jnp.where((lane >= row) & (lane < SNAPS), scaled, 0.0)
        lower.append(jnp.where(row < SNAPS, pltpu.roll(scaled, 64, 1), 0.0))
    lower = jnp.concatenate(lower, axis=0)[:, :64]
    stacked = jnp.concatenate(split3(lower), axis=0)

    def modes_step(i, carry):
        parts = jnp.dot(stacked, snap_b[i], preferred_element_type=f32)
        both = parts[0:64] + (parts[64:128] + parts[128:192])
        for half in range(2):
            flat_modes[pl.ds(2 * i + half, 64, stride=BLOCKS), :] = both[:, 128 * half : 128 * half + 128]
        return carry

    lax.fori_loop(0, BLOCKS // 2, modes_step, 0)
    store_modes = pltpu.make_async_copy(
        flat_modes.at[pl.ds(0, SNAPS * BLOCKS)], out_modes.at[pl.ds(0, SNAPS * BLOCKS)], store_sem.at[6]
    )
    store_modes.start()

    loop(4, X, lambda x: second_layer(state, state2, prim2, updated, sums, x))
    for copy in far_copies:
        copy.wait()
    loop(0, 2, lambda i: primitive_layer(state, prim, 11 * i))
    loop(0, 2, lambda i: first_layer(state, prim, state2, prim2, 1 + 9 * i))
    loop(2, 4, lambda x: second_layer(state, state2, prim2, updated, sums, x))
    loop(X, 2 + X, lambda x: second_layer(state, state2, prim2, updated, sums, x))
    stores = [store_modes]
    for t in range(2):
        lanes = pl.ds(128 * t, 128)
        stores += [
            pltpu.make_async_copy(updated.at[0, :, t], out_density.at[:, :, lanes], store_sem.at[3 * t]),
            pltpu.make_async_copy(updated.at[pl.ds(1, 3), :, t], out_momentum.at[:, :, :, lanes], store_sem.at[3 * t + 1]),
            pltpu.make_async_copy(updated.at[4, :, t], out_energy.at[:, :, lanes], store_sem.at[3 * t + 2]),
        ]
    for copy in stores[1:]:
        copy.start()

    flat_sums = flat(sums)
    columns = []
    for half in range(2):
        for t in range(2):
            parts = []
            for c in range(6):
                start = (c * 2 + t) * Y + 4 * half
                part = flat_sums[pl.ds(start, 8, stride=8), :]
                for k in range(1, 4):
                    part = part + flat_sums[pl.ds(start + k, 8, stride=8), :]
                parts.append(part)
            columns.append(jnp.concatenate(parts, axis=0))
    fine = jnp.concatenate(columns, axis=1)
    source = lax.broadcasted_iota(jnp.int32, (512, 128), 0)
    target = lax.broadcasted_iota(jnp.int32, (512, 128), 1)
    gather = jnp.where(lax.shift_right_logical(source, 2) == target, 1.0 / 64.0, 0.0).astype(bf16)
    means = sum(jnp.dot(part, gather, preferred_element_type=f32) for part in split3(fine))
    for c in range(3):
        for half in range(2):
            first = (2 * c + half) * 8
            coarse[pl.ds(16 * c + half, 8, stride=2), :] = means[first : first + 8]

    def dot_step(i, acc):
        for part in range(4):
            b = 4 * i + part
            acc = acc + flat_modes[pl.ds(b, 64, stride=BLOCKS), :] * coarse[pl.ds(b, 1), :]
        return acc

    acc = lax.fori_loop(0, BLOCKS // 4, dot_step, jnp.zeros((64, 128), f32))
    squares = jnp.sum(coarse[...] * coarse[...], axis=0, keepdims=True)
    acc = jnp.where(lax.broadcasted_iota(jnp.int32, (64, 128), 0) == SNAPS, squares, acc)
    ones = jnp.ones((8, 128), bf16)
    products = sum(
        lax.dot_general(ones, part, (((1,), (1,)), ((), ())), preferred_element_type=f32) for part in split3(acc)
    )
    dot_sums[0] = jnp.concatenate([products, jnp.zeros((8, 64), f32)], axis=1)
    stages = ((dot_gy, gy, n_gy, on_gy, 0), (dot_z, iz, n_z, on_z, 8), (dot_y, iy, n_y, on_y, 16))
    for stage, (target, me, count, device_of, first) in enumerate(stages):
        copies = exchange(lambda peer: dot_sums.at[stage], target, me, count, device_of, dot_send, dot_recv, first)
        target[me] = dot_sums[stage]
        for copy in copies:
            copy.wait()
        dot_sums[stage + 1] = total(target, count)
    share = dot_sums[3] / rows_all

    rest = jnp.where(lane < SNAPS, share, 0.0)
    norm = jnp.sum(jnp.where(lane == SNAPS, share, 0.0), axis=1, keepdims=True)
    last = jnp.sqrt(norm - jnp.sum(rest * rest, axis=1, keepdims=True))
    for b in range(8):
        row = sub + 8 * b
        column = jnp.sum(jnp.where(lane == row, rest, 0.0), axis=1, keepdims=True)
        column = jnp.where(row == SNAPS, last, column)
        out_factor[8 * b : 8 * b + 8, :] = jnp.where(lane == SNAPS, column, factor_v[b])[:, :64]
    mode = [coarse[8 * i : 8 * i + 8, :] for i in range(6)]
    for m in range(SNAPS):
        weight = jnp.broadcast_to(rest[:, m : m + 1], (8, 128))
        for i in range(6):
            mode[i] = mode[i] - weight * flat_modes[BLOCKS * m + 8 * i : BLOCKS * m + 8 * i + 8, :]
    scale = 1.0 / last
    for i in range(6):
        flat_modes[BLOCKS * SNAPS + 8 * i : BLOCKS * SNAPS + 8 * i + 8, :] = mode[i] * scale
    store_last = pltpu.make_async_copy(
        flat_modes.at[pl.ds(SNAPS * BLOCKS, BLOCKS)], out_modes.at[pl.ds(SNAPS * BLOCKS, BLOCKS)], store_sem.at[7]
    )
    store_last.start()
    for copy in stores + [store_last]:
        copy.wait()


def solution(mesh):
    n_gx, n_gy = mesh.shape["gx"], mesh.shape["gy"]
    n_y = 4
    n_z = n_gx // n_y

    def on_device(density, momentum, energy, snapshots):
        rows_all = 6144 * n_gx * n_gy
        snapshots = snapshots.reshape(SNAPS, 3, 2, 8, 128).transpose(0, 1, 3, 2, 4).reshape(SNAPS, 3, 16, 128)
        anywhere = pl.BlockSpec(memory_space=pl.ANY)
        vmem = pl.BlockSpec(memory_space=pltpu.VMEM)
        dma = pltpu.SemaphoreType.DMA
        new_density, new_momentum, new_energy, factor, modes = pl.pallas_call(
            functools.partial(kernel, float(rows_all), (n_gx, n_gy, n_y)),
            name="sections_and_modes",
            in_specs=[anywhere] * 4,
            out_specs=(anywhere, anywhere, anywhere, vmem, anywhere),
            out_shape=(
                jax.ShapeDtypeStruct((X, Y, Z), f32),
                jax.ShapeDtypeStruct((3, X, Y, Z), f32),
                jax.ShapeDtypeStruct((X, Y, Z), f32),
                jax.ShapeDtypeStruct((64, 64), f32),
                jax.ShapeDtypeStruct((64 * BLOCKS, 128), f32),
            ),
            scratch_shapes=[
                pltpu.VMEM((5, XP, 2, YP, 128), f32),
                pltpu.VMEM((4, XP, 2, YP, 128), f32),
                pltpu.VMEM((5, XP, 2, YP, 128), f32),
                pltpu.VMEM((4, XP, 2, YP, 128), f32),
                pltpu.VMEM((5, X, 2, Y, 128), f32),
                pltpu.VMEM((3, 2, 2, Y, 128), f32),
                pltpu.VMEM((2, 5, 2, 2, 8, 128), f32),
                pltpu.VMEM((2, 5, 2, 2, 8, 128), f32),
                pltpu.VMEM((2, 2, 2, 8, 128), f32),
                pltpu.VMEM((2, 2, 2, 8, 128), f32),
                pltpu.VMEM((SNAPS, 3, 16, 128), bf16),
                pltpu.VMEM((64, 3, 16, 128), f32),
                pltpu.VMEM((BLOCKS // 2, 64, 256), bf16),
                pltpu.VMEM((64, 3, 16, 128), f32),
                pltpu.VMEM((8, 8, 128), f32),
                pltpu.VMEM((BLOCKS, 128), f32),
                pltpu.VMEM((8, 8, 128), f32),
                pltpu.VMEM((n_gy, 8, 128), f32),
                pltpu.VMEM((n_z, 8, 128), f32),
                pltpu.VMEM((n_y, 8, 128), f32),
                pltpu.VMEM((8, 8, 128), f32),
                pltpu.VMEM((3, 8, 128), f32),
                pltpu.VMEM((n_gy, 8, 128), f32),
                pltpu.VMEM((n_z, 8, 128), f32),
                pltpu.VMEM((n_y, 8, 128), f32),
                pltpu.VMEM((4, 8, 128), f32),
                dma((7,)),
                dma((8,)),
                dma((24,)),
                dma((24,)),
                dma((2,)),
                dma((2,)),
                dma((4,)),
                dma((4,)),
                dma((32,)),
                dma((32,)),
                dma((24,)),
                dma((24,)),
            ],
            compiler_params=pltpu.CompilerParams(
                collective_id=0, has_side_effects=True, vmem_limit_bytes=32 * 2**20
            ),
        )(density, momentum, energy, snapshots)
        modes = modes.reshape(64, 3, 8, 2, 128).transpose(0, 1, 3, 2, 4).reshape(64, 3, 2, 1024)
        return new_density, new_momentum, new_energy, factor, modes

    placed = (
        P("gx", "gy", None),
        P(None, "gx", "gy", None),
        P("gx", "gy", None),
        P(None, None, "gx", "gy"),
    )
    return jax.shard_map(
        on_device,
        mesh=mesh,
        in_specs=placed,
        out_specs=(
            P("gx", "gy", None),
            P(None, "gx", "gy", None),
            P("gx", "gy", None),
            P(),
            P(None, None, "gx", "gy"),
        ),
        check_vma=False,
    )
```

```python
import functools

import jax
import jax.numpy as jnp
from jax import lax
from jax.experimental import pallas as pl
from jax.experimental.pallas import tpu as pltpu
from jax.sharding import PartitionSpec as P

f32 = jnp.float32
bf16 = jnp.bfloat16
MESH = pl.DeviceIdType.MESH

time_step = 0.08
shear_friction_coefficient = 1.5
heat_conduction_coefficient = 1.5

X, Y, Z = 8, 64, 256
XP, YP = 12, 80
STEP_X = 2 * YP
SNAPS = 63
BLOCKS = 48
CHUNK = 32
UNROLL = 4
FAR_AT = 0
SPLIT = 24


def flat(ref):
    rows = 1
    for size in ref.shape[:-1]:
        rows *= size
    return ref.reshape(rows, 128)


def split3(value):
    high = value.astype(bf16)
    rest = value - high.astype(f32)
    middle = rest.astype(bf16)
    low = (rest - middle.astype(f32)).astype(bf16)
    return high, middle, low


def z_pair(pair, copied):
    low, high = pair
    lane = lax.broadcasted_iota(jnp.int32, low.shape, 1)
    last, first = lane == 127, lane == 0
    low_up, high_up = pltpu.roll(low, 127, 1), pltpu.roll(high, 127, 1)
    low_down, high_down = pltpu.roll(low, 1, 1), pltpu.roll(high, 1, 1)
    above, below = (high, low) if copied else (0.0, 0.0)
    up = (jnp.where(last, high_up, low_up), jnp.where(last, above, high_up))
    down = (jnp.where(first, below, low_down), jnp.where(first, low_down, high_down))
    return up, down


def primitives(state):
    inverse = 1.0 / state[0]
    return [state[1 + field] * inverse for field in range(4)]


def change(center, x_up, x_down, y_up, y_down, mx_up, mx_down, my_up, my_down, mz):
    up, down = z_pair(mz, False)
    result = [
        [
            (-0.5 * time_step) * ((mx_up[t] - mx_down[t]) + (my_up[t] - my_down[t]) + (up[t] - down[t]))
            for t in range(2)
        ]
    ]
    for field in range(4):
        rate = heat_conduction_coefficient if field == 3 else shear_friction_coefficient
        up, down = z_pair(center[field], field == 3)
        result.append(
            [
                (time_step * rate)
                * (
                    (x_up[field][t] + x_down[field][t])
                    + (y_up[field][t] + y_down[field][t])
                    + (up[t] + down[t])
                    - 6.0 * center[field][t]
                )
                for t in range(2)
            ]
        )
    return result


def change_rows(prim, state, x, row, count):
    def v(dx, dy):
        return [[prim[f, x + dx, t, pl.ds(row + dy, count), :] for t in range(2)] for f in range(4)]

    def s(field, dx, dy):
        return [state[field, x + dx, t, pl.ds(row + dy, count), :] for t in range(2)]

    return change(
        v(0, 0), v(1, 0), v(-1, 0), v(0, 1), v(0, -1),
        s(1, 1, 0), s(1, -1, 0), s(2, 0, 1), s(2, 0, -1), s(3, 0, 0),
    )


def primitive_layer(state, prim, x):
    for row in range(8, 8 + Y, CHUNK):
        for t in range(2):
            values = primitives([state[f, x, t, pl.ds(row, CHUNK), :] for f in range(5)])
            for f in range(4):
                prim[f, x, t, pl.ds(row, CHUNK), :] = values[f]


def first_layer(state, prim, state2, prim2, x):
    for row in range(8, 8 + Y, CHUNK):
        delta = change_rows(prim, state, x, row, CHUNK)
        for t in range(2):
            new = [state[f, x, t, pl.ds(row, CHUNK), :] + delta[f][t] for f in range(5)]
            values = primitives(new)
            for f in range(5):
                state2[f, x, t, pl.ds(row, CHUNK), :] = new[f]
            for f in range(4):
                prim2[f, x, t, pl.ds(row, CHUNK), :] = values[f]


def second_layer(state, state2, prim2, updated, sums, x):
    for row in range(8, 8 + Y, CHUNK):
        delta = change_rows(prim2, state2, x, row, CHUNK)
        for t in range(2):
            new = [
                0.5 * state[f, x, t, pl.ds(row, CHUNK), :]
                + 0.5 * (state2[f, x, t, pl.ds(row, CHUNK), :] + delta[f][t])
                for f in range(5)
            ]
            inverse = 1.0 / new[0]
            for f in range(5):
                updated[f, x - 2, t, pl.ds(row - 8, CHUNK), :] = new[f]
            for c in range(3):
                sums[c, (x - 2) // 4, t, pl.ds(row - 8, CHUNK), :] += new[1 + c] * inverse


def sheet(field, tile, row, dx=0):
    return pl.ds(((field * XP + 2 + dx) * 2 + tile) * YP + row, X, stride=STEP_X)


def place_rows(state, prim, y_in, side):
    row = 7 if side == 0 else 72
    flat_state, flat_prim = flat(state), flat(prim)
    for t in range(2):
        near = [y_in[side, f, 0, t] for f in range(5)]
        values = primitives(near)
        for f in range(4):
            flat_prim[sheet(f, t, row), :] = values[f]
        for f in (1, 2):
            flat_state[sheet(f, t, row), :] = near[f]


def place_corner(state, prim, corner_in, side_x, side_y):
    x = 1 if side_x == 0 else 10
    row = 7 if side_y == 0 else 72
    for t in range(2):
        values = corner_in[side_x, side_y, t]
        inverse = 1.0 / values[0:1]
        for f in range(4):
            prim[f, x, t, pl.ds(row, 1), :] = values[1 + f : 2 + f] * inverse
        for f in (1, 2):
            state[f, x, t, pl.ds(row, 1), :] = values[f : f + 1]


def edge_rows(state, prim, state2, prim2, y_in, side):
    row, own = (7, 8) if side == 0 else (72, 71)
    flat_state, flat_prim = flat(state), flat(prim)
    flat_state2, flat_prim2 = flat(state2), flat(prim2)

    def v(at, dx):
        return [[flat_prim[sheet(f, t, at, dx), :] for t in range(2)] for f in range(4)]

    def s(field, at, dx):
        return [flat_state[sheet(field, t, at, dx), :] for t in range(2)]

    near = [[y_in[side, f, 0, t] for f in range(5)] for t in range(2)]
    far = [primitives([y_in[side, f, 1, t] for f in range(5)]) for t in range(2)]
    far = [[far[t][f] for t in range(2)] for f in range(4)]
    far_my = [y_in[side, 2, 1, t] for t in range(2)]
    inner, inner_my = v(own, 0), s(2, own, 0)
    y_up, y_down, my_up, my_down = (
        (inner, far, inner_my, far_my) if side == 0 else (far, inner, far_my, inner_my)
    )
    delta = change(
        v(row, 0), v(row, 1), v(row, -1), y_up, y_down,
        s(1, row, 1), s(1, row, -1), my_up, my_down, [near[t][3] for t in range(2)],
    )
    for t in range(2):
        new = [near[t][f] + delta[f][t] for f in range(5)]
        values = primitives(new)
        for f in range(4):
            flat_prim2[sheet(f, t, row), :] = values[f]
        flat_state2[sheet(2, t, row), :] = new[2]


def eliminate(rows, first, stop):
    sub = lax.broadcasted_iota(jnp.int32, (8, 128), 0)

    def along_lanes(value, k):
        return jnp.broadcast_to(value[:, k : k + 1], (8, 128))

    def along_rows(value, k):
        return jnp.broadcast_to(value[k : k + 1, :], (8, 128))

    for k in range(first, stop, 2):
        block, at = divmod(k, 8)
        left = {b: along_lanes(rows[b], k) for b in range(block, 8)}
        right = {b: along_lanes(rows[b], k + 1) for b in range(block, 8)}
        cross = along_rows(left[block], at + 1)
        inverse = 1.0 / along_rows(left[block], at)
        ratio = cross * inverse
        pivot = along_rows(right[block], at + 1) - ratio * cross
        row = along_rows(rows[block], at)
        next_row = along_rows(rows[block], at + 1) - ratio * row
        row = row * inverse
        next_row = next_row * (1.0 / pivot)
        for b in range(block, 8):
            first_column, second_column = left[b], right[b] - ratio * left[b]
            if b == block:
                first_column = jnp.where(sub > at, first_column, 0.0)
                second_column = jnp.where(sub > at + 1, second_column, 0.0)
            rows[b] = rows[b] - first_column * row - second_column * next_row
    return rows


def kernel(
    rows_all, sizes,
    density, momentum, energy, snapshots,
    out_density, out_momentum, out_energy, out_factor, out_modes,
    state, prim, state2, prim2, updated, sums,
    y_out, y_in, corner_out, corner_in,
    snap_in, snap_f, snap_b, modes, factor_v, lower_v, coarse,
    gram, gram_part, gram_z, gram_y, gram_all, gram_sums,
    dot_gy, dot_z, dot_y, dot_sums,
    load_sem, store_sem,
    x_send, x_recv, y_send, y_recv, corner_send, corner_recv,
    gram_send, gram_recv, dot_send, dot_recv,
):
    n_gx, n_gy, n_y = sizes
    n_z = n_gx // n_y
    gx, gy = lax.axis_index("gx"), lax.axis_index("gy")
    iz, iy = lax.div(gx, n_y), lax.rem(gx, n_y)

    def moved(dx, dy):
        return {"gx": lax.rem(gx + dx + n_gx, n_gx), "gy": lax.rem(gy + dy + n_gy, n_gy)}

    def on_gy(i):
        return {"gx": gx, "gy": i}

    def on_z(i):
        return {"gx": i * n_y + iy, "gy": gy}

    def on_y(i):
        return {"gx": iz * n_y + i, "gy": gy}

    loads = []
    for t in range(2):
        lanes, rows = pl.ds(128 * t, 128), pl.ds(8, Y)
        loads += [
            pltpu.make_async_copy(density.at[:, :, lanes], state.at[0, pl.ds(2, X), t, rows, :], load_sem.at[3 * t]),
            pltpu.make_async_copy(
                momentum.at[:, :, :, lanes], state.at[pl.ds(1, 3), pl.ds(2, X), t, rows, :], load_sem.at[3 * t + 1]
            ),
            pltpu.make_async_copy(energy.at[:, :, lanes], state.at[4, pl.ds(2, X), t, rows, :], load_sem.at[3 * t + 2]),
        ]
    load_snapshots = pltpu.make_async_copy(snapshots, snap_in, load_sem.at[6])
    for copy in loads:
        copy.start()
    load_snapshots.start()

    barrier = pltpu.get_barrier_semaphore()
    greeted = [moved(dx, dy) for dx in (-1, 1) for dy in (-1, 0, 1)]
    greeted += [on_gy(lax.rem(gy + d, n_gy)) for d in range(1, n_gy)]
    greeted += [on_z(lax.rem(iz + d, n_z)) for d in range(1, n_z)]
    greeted += [on_y(lax.rem(iy + d, n_y)) for d in range(1, n_y)]
    for device in greeted:
        pl.semaphore_signal(barrier, inc=1, device_id=device, device_id_type=MESH)
    pl.semaphore_wait(barrier, len(greeted))

    def remote(source, target, send_sem, recv_sem, device):
        return pltpu.make_async_remote_copy(
            src_ref=source, dst_ref=target, send_sem=send_sem, recv_sem=recv_sem, device_id=device, device_id_type=MESH
        )

    def x_copies(layer):
        copies = []
        for side in range(2):
            source, target = (X - 1 - layer, 1 - layer) if side == 0 else (layer, 10 + layer)
            device = moved(1, 0) if side == 0 else moved(-1, 0)
            for t in range(2):
                lanes, rows = pl.ds(128 * t, 128), pl.ds(8, Y)
                at = ((layer * 2 + side) * 2 + t) * 3
                copies += [
                    remote(
                        density.at[source, :, lanes], state.at[0, target, t, rows, :],
                        x_send.at[at], x_recv.at[at], device,
                    ),
                    remote(
                        momentum.at[:, source, :, lanes], state.at[pl.ds(1, 3), target, t, rows, :],
                        x_send.at[at + 1], x_recv.at[at + 1], device,
                    ),
                    remote(
                        energy.at[source, :, lanes], state.at[4, target, t, rows, :],
                        x_send.at[at + 2], x_recv.at[at + 2], device,
                    ),
                ]
        return copies

    def start(copies):
        for copy in copies:
            copy.start()

    def wait(copies):
        for copy in copies:
            copy.wait()

    def loop(first, stop, step):
        lax.fori_loop(first, stop, lambda x, _: (step(x), 0)[1], 0)

    def exchange(sources, target, me, count, device_of, send, recv, first):
        copies = []
        for d in sorted(range(1, count), key=lambda d: -min(d, count - d)):
            peer = lax.rem(me + d, count)
            copies.append(
                remote(sources(peer), target.at[me], send.at[first + d], recv.at[first + d], device_of(peer))
            )
        start(copies)
        return copies

    def total(ref, count):
        value = ref[0]
        for i in range(1, count):
            value = value + ref[i]
        return value

    near_copies, far_copies = x_copies(0), x_copies(1)
    start(near_copies)

    load_snapshots.wait()
    for c in range(3):
        snap_f[0:SNAPS, c] = snap_in[:, c].astype(f32)
    snap_f[SNAPS] = jnp.zeros((3, 16, 128), f32)
    flat_snap, flat_modes = flat(snap_f), flat(modes)

    def gram_step(i, value):
        for part in range(UNROLL):
            at = UNROLL * i + part
            pair = [flat_snap[pl.ds(2 * at + half, 64, stride=BLOCKS), :] for half in range(2)]
            pair = jnp.concatenate(pair, axis=1).astype(bf16)
            snap_b[at] = pair
            value = value + lax.dot_general(pair, pair, (((1,), (1,)), ((), ())), preferred_element_type=f32)
        return value

    local = lax.fori_loop(0, BLOCKS // 2 // UNROLL, gram_step, jnp.zeros((64, 64), f32))
    local = jnp.concatenate([local, jnp.zeros((64, 64), f32)], axis=1)
    for b in range(8):
        gram[b] = local[8 * b : 8 * b + 8]
    scatter = exchange(lambda peer: gram.at[peer], gram_part, gy, n_gy, on_gy, gram_send, gram_recv, 0)
    gram_part[gy] = gram[gy]

    wait(loads)
    flat_state = flat(state)
    for side in range(2):
        for f in range(5):
            for far in range(2):
                y = Y - 1 - far if side == 0 else far
                for t in range(2):
                    y_out[side, f, far, t] = flat_state[sheet(f, t, 8 + y), :]
    y_copies = [
        remote(y_out.at[side], y_in.at[side], y_send.at[side], y_recv.at[side], moved(0, 1 - 2 * side))
        for side in range(2)
    ]
    start(y_copies)
    corner_out[...] = jnp.zeros_like(corner_out)
    corner_copies = []
    for side_x in range(2):
        for side_y in range(2):
            x, y = (X - 1) * (1 - side_x), (Y - 1) * (1 - side_y)
            for t in range(2):
                begin = ((2 + x) * 2 + t) * YP + 8 + y
                corner_out[side_x, side_y, t, 0:5] = flat_state[pl.ds(begin, 5, stride=XP * STEP_X), :]
            at = side_x * 2 + side_y
            corner_copies.append(
                remote(
                    corner_out.at[side_x, side_y], corner_in.at[side_x, side_y],
                    corner_send.at[at], corner_recv.at[at], moved(1 - 2 * side_x, 1 - 2 * side_y),
                )
            )
    start(corner_copies)
    if FAR_AT == 0:
        start(far_copies)

    loop(2, 2 + X, lambda x: primitive_layer(state, prim, x))
    wait(scatter)
    gram_sums[0] = total(gram_part, n_gy)
    copies = exchange(lambda peer: gram_sums.at[0], gram_z, iz, n_z, on_z, gram_send, gram_recv, 8)
    gram_z[iz] = gram_sums[0]
    if FAR_AT == 1:
        start(far_copies)
    wait(y_copies)
    for side in range(2):
        place_rows(state, prim, y_in, side)
    loop(3, 1 + X, lambda x: first_layer(state, prim, state2, prim2, x))
    sums[...] = jnp.zeros_like(sums)
    wait(copies)
    gram_sums[1] = total(gram_z, n_z)
    copies = exchange(lambda peer: gram_sums.at[1], gram_y, iy, n_y, on_y, gram_send, gram_recv, 16)
    gram_y[iy] = gram_sums[1]
    if FAR_AT == 2:
        start(far_copies)
    wait(near_copies + corner_copies)
    loop(0, 2, lambda i: primitive_layer(state, prim, 1 + 9 * i))
    for side_x in range(2):
        for side_y in range(2):
            place_corner(state, prim, corner_in, side_x, side_y)
    loop(0, 2, lambda i: first_layer(state, prim, state2, prim2, 2 + 7 * i))
    for side in range(2):
        edge_rows(state, prim, state2, prim2, y_in, side)
    wait(copies)
    gram_sums[2] = total(gram_y, n_y)
    gather = exchange(lambda peer: gram_sums.at[2], gram_all, gy, n_gy, on_gy, gram_send, gram_recv, 24)
    gram_all[gy] = gram_sums[2]
    loop(3, 1 + X, lambda x: second_layer(state, state2, prim2, updated, sums, x))
    wait(far_copies)
    loop(0, 2, lambda i: primitive_layer(state, prim, 11 * i))
    loop(0, 2, lambda i: first_layer(state, prim, state2, prim2, 1 + 9 * i))
    loop(0, 2, lambda i: second_layer(state, state2, prim2, updated, sums, 2 + 7 * i))

    flat_sums = flat(sums)
    columns = []
    for half in range(2):
        for t in range(2):
            parts = []
            for c in range(6):
                begin = (c * 2 + t) * Y + 4 * half
                part = flat_sums[pl.ds(begin, 8, stride=8), :]
                for k in range(1, 4):
                    part = part + flat_sums[pl.ds(begin + k, 8, stride=8), :]
                parts.append(part)
            columns.append(jnp.concatenate(parts, axis=0))
    fine = jnp.concatenate(columns, axis=1)
    source = lax.broadcasted_iota(jnp.int32, (512, 128), 0)
    target = lax.broadcasted_iota(jnp.int32, (512, 128), 1)
    selection = jnp.where(lax.shift_right_logical(source, 2) == target, 1.0 / 64.0, 0.0).astype(bf16)
    means = sum(jnp.dot(part, selection, preferred_element_type=f32) for part in split3(fine))
    for c in range(3):
        for half in range(2):
            at = (2 * c + half) * 8
            coarse[pl.ds(16 * c + half, 8, stride=2), :] = means[at : at + 8]

    def dot_step(i, acc):
        for part in range(4):
            b = 4 * i + part
            acc = acc + flat_snap[pl.ds(b, 64, stride=BLOCKS), :] * coarse[pl.ds(b, 1), :]
        return acc

    acc = lax.fori_loop(0, BLOCKS // 4, dot_step, jnp.zeros((64, 128), f32))
    squares = jnp.sum(coarse[...] * coarse[...], axis=0, keepdims=True)
    acc = jnp.where(lax.broadcasted_iota(jnp.int32, (64, 128), 0) == SNAPS, squares, acc)
    ones = jnp.ones((8, 128), bf16)
    products = sum(
        lax.dot_general(ones, part, (((1,), (1,)), ((), ())), preferred_element_type=f32) for part in split3(acc)
    )
    dot_sums[0] = jnp.concatenate([products, jnp.zeros((8, 64), f32)], axis=1)
    copies = exchange(lambda peer: dot_sums.at[0], dot_gy, gy, n_gy, on_gy, dot_send, dot_recv, 0)
    dot_gy[gy] = dot_sums[0]

    stores = []
    for t in range(2):
        lanes = pl.ds(128 * t, 128)
        stores += [
            pltpu.make_async_copy(updated.at[0, :, t], out_density.at[:, :, lanes], store_sem.at[3 * t]),
            pltpu.make_async_copy(updated.at[pl.ds(1, 3), :, t], out_momentum.at[:, :, :, lanes], store_sem.at[3 * t + 1]),
            pltpu.make_async_copy(updated.at[4, :, t], out_energy.at[:, :, lanes], store_sem.at[3 * t + 2]),
        ]
    start(stores)
    wait(gather)
    lane = lax.broadcasted_iota(jnp.int32, (8, 128), 1)
    sub = lax.broadcasted_iota(jnp.int32, (8, 128), 0)
    blocks = []
    for b in range(8):
        row = sub + 8 * b
        known = (row < SNAPS) & (lane < SNAPS)
        unit = ((lane == row) & (row == SNAPS)) | (lane == row + 64)
        blocks.append(jnp.where(known, gram_all[b] / rows_all, jnp.where(unit, 1.0, 0.0)))
    blocks = eliminate(blocks, 0, SPLIT)
    wait(copies)
    dot_sums[1] = total(dot_gy, n_gy)
    copies = exchange(lambda peer: dot_sums.at[1], dot_z, iz, n_z, on_z, dot_send, dot_recv, 8)
    dot_z[iz] = dot_sums[1]
    blocks = eliminate(blocks, SPLIT, SNAPS - 1)
    for b in range(8):
        row = sub + 8 * b
        diagonal = jnp.sum(jnp.where(lane == row, blocks[b], 0.0), axis=1, keepdims=True)
        scaled = blocks[b] * (1.0 / jnp.sqrt(diagonal))
        factor_v[b] = jnp.where((lane >= row) & (lane < SNAPS), scaled, 0.0)
        lower_v[b] = jnp.where((row < SNAPS) & (lane < 64), pltpu.roll(scaled, 64, 1), 0.0)
    wait(copies)
    dot_sums[2] = total(dot_z, n_z)
    copies = exchange(lambda peer: dot_sums.at[2], dot_y, iy, n_y, on_y, dot_send, dot_recv, 16)
    dot_y[iy] = dot_sums[2]
    stacked = jnp.concatenate(split3(lower_v[...].reshape(64, 128)[:, :64]), axis=0)

    def modes_step(i, carry):
        for part in range(UNROLL):
            at = UNROLL * i + part
            parts = jnp.dot(stacked, snap_b[at], preferred_element_type=f32)
            both = parts[0:64] + (parts[64:128] + parts[128:192])
            for half in range(2):
                flat_modes[pl.ds(2 * at + half, 64, stride=BLOCKS), :] = both[:, 128 * half : 128 * half + 128]
        return carry

    lax.fori_loop(0, BLOCKS // 2 // UNROLL, modes_step, 0)
    store_modes = pltpu.make_async_copy(
        flat_modes.at[pl.ds(0, SNAPS * BLOCKS)], out_modes.at[pl.ds(0, SNAPS * BLOCKS)], store_sem.at[6]
    )
    store_modes.start()
    wait(copies)
    share = total(dot_y, n_y) / rows_all

    own = jnp.where(lane < SNAPS, share, 0.0)
    left = jnp.sum(jnp.where(lane == SNAPS, share, 0.0), axis=1, keepdims=True)[0:1]
    weights = []
    for b in range(8):
        weights.append(jnp.sum(lower_v[b] * own, axis=1, keepdims=True))
        left = left - jnp.sum(weights[b] * weights[b], axis=0, keepdims=True)
    last = jnp.broadcast_to(jnp.sqrt(left), (8, 128))
    mode = [coarse[8 * i : 8 * i + 8, :] for i in range(6)]
    for b in range(8):
        row = sub + 8 * b
        weight = jnp.broadcast_to(weights[b], (8, 128))
        column = jnp.where(row == SNAPS, last, weight)
        out_factor[8 * b : 8 * b + 8, :] = jnp.where(lane == SNAPS, column, factor_v[b])[:, :64]
        for at in range(8 if b < 7 else 7):
            one = jnp.broadcast_to(weight[at : at + 1], (8, 128))
            begin = BLOCKS * (8 * b + at)
            for i in range(6):
                mode[i] = mode[i] - one * flat_modes[begin + 8 * i : begin + 8 * i + 8, :]
    scale = 1.0 / last
    for i in range(6):
        flat_modes[BLOCKS * SNAPS + 8 * i : BLOCKS * SNAPS + 8 * i + 8, :] = mode[i] * scale
    store_last = pltpu.make_async_copy(
        flat_modes.at[pl.ds(SNAPS * BLOCKS, BLOCKS)], out_modes.at[pl.ds(SNAPS * BLOCKS, BLOCKS)], store_sem.at[7]
    )
    store_last.start()
    wait(stores + [store_modes, store_last])


def copy_out(*refs):
    sources, targets, sem = refs[:5], refs[5:10], refs[10]
    copies = []
    for i, (source, target) in enumerate(zip(sources, targets)):
        if source.ndim == 4:
            copies += [pltpu.make_async_copy(source.at[c], target.at[c], sem.at[5 + c]) for c in range(3)]
        else:
            copies.append(pltpu.make_async_copy(source, target, sem.at[i]))
    for copy in copies:
        copy.start()
    for copy in copies:
        copy.wait()


def solution(mesh):
    n_gx, n_gy = mesh.shape["gx"], mesh.shape["gy"]
    n_y = 4
    n_z = n_gx // n_y

    def on_device(density, momentum, energy, snapshots):
        rows_all = 6144 * n_gx * n_gy
        snapshots = snapshots.reshape(SNAPS, 3, 2, 8, 128).transpose(0, 1, 3, 2, 4).reshape(SNAPS, 3, 16, 128)
        anywhere = pl.BlockSpec(memory_space=pl.ANY)
        vmem = pl.BlockSpec(memory_space=pltpu.VMEM)
        dma = pltpu.SemaphoreType.DMA
        results = pl.pallas_call(
            functools.partial(kernel, float(rows_all), (n_gx, n_gy, n_y)),
            name="sections_and_modes",
            in_specs=[pl.BlockSpec(memory_space=pltpu.HBM)] * 4,
            out_specs=(anywhere, anywhere, anywhere, vmem, anywhere),
            out_shape=(
                jax.ShapeDtypeStruct((X, Y, Z), f32),
                jax.ShapeDtypeStruct((3, X, Y, Z), f32),
                jax.ShapeDtypeStruct((X, Y, Z), f32),
                jax.ShapeDtypeStruct((64, 64), f32),
                jax.ShapeDtypeStruct((64 * BLOCKS, 128), f32),
            ),
            scratch_shapes=[
                pltpu.VMEM((5, XP, 2, YP, 128), f32),
                pltpu.VMEM((4, XP, 2, YP, 128), f32),
                pltpu.VMEM((5, XP, 2, YP, 128), f32),
                pltpu.VMEM((4, XP, 2, YP, 128), f32),
                pltpu.VMEM((5, X, 2, Y, 128), f32),
                pltpu.VMEM((3, 2, 2, Y, 128), f32),
                pltpu.VMEM((2, 5, 2, 2, 8, 128), f32),
                pltpu.VMEM((2, 5, 2, 2, 8, 128), f32),
                pltpu.VMEM((2, 2, 2, 8, 128), f32),
                pltpu.VMEM((2, 2, 2, 8, 128), f32),
                pltpu.VMEM((SNAPS, 3, 16, 128), bf16),
                pltpu.VMEM((64, 3, 16, 128), f32),
                pltpu.VMEM((BLOCKS // 2, 64, 256), bf16),
                pltpu.VMEM((64, 3, 16, 128), f32),
                pltpu.VMEM((8, 8, 128), f32),
                pltpu.VMEM((8, 8, 128), f32),
                pltpu.VMEM((BLOCKS, 128), f32),
                pltpu.VMEM((8, 8, 128), f32),
                pltpu.VMEM((n_gy, 8, 128), f32),
                pltpu.VMEM((n_z, 8, 128), f32),
                pltpu.VMEM((n_y, 8, 128), f32),
                pltpu.VMEM((8, 8, 128), f32),
                pltpu.VMEM((3, 8, 128), f32),
                pltpu.VMEM((n_gy, 8, 128), f32),
                pltpu.VMEM((n_z, 8, 128), f32),
                pltpu.VMEM((n_y, 8, 128), f32),
                pltpu.VMEM((4, 8, 128), f32),
                dma((7,)),
                dma((8,)),
                dma((24,)),
                dma((24,)),
                dma((2,)),
                dma((2,)),
                dma((4,)),
                dma((4,)),
                dma((32,)),
                dma((32,)),
                dma((24,)),
                dma((24,)),
            ],
            compiler_params=pltpu.CompilerParams(
                collective_id=0, has_side_effects=True, vmem_limit_bytes=32 * 2**20
            ),
        )(*(pltpu.with_memory_space_constraint(a, pltpu.HBM) for a in (density, momentum, energy, snapshots)))
        new_density, new_momentum, new_energy, factor, modes = pl.pallas_call(
            copy_out,
            name="copy_out",
            in_specs=[anywhere] * 5,
            out_specs=[pl.BlockSpec(memory_space=pltpu.HBM)] * 5,
            out_shape=[jax.ShapeDtypeStruct(value.shape, f32) for value in results],
            scratch_shapes=[dma((8,))],
            compiler_params=pltpu.CompilerParams(vmem_limit_bytes=2**20),
        )(*results)
        modes = modes.reshape(64, 3, 8, 2, 128).transpose(0, 1, 3, 2, 4).reshape(64, 3, 2, 1024)
        return new_density, new_momentum, new_energy, factor, modes

    placed = (
        P("gx", "gy", None),
        P(None, "gx", "gy", None),
        P("gx", "gy", None),
        P(None, None, "gx", "gy"),
    )
    return jax.shard_map(
        on_device,
        mesh=mesh,
        in_specs=placed,
        out_specs=(
            P("gx", "gy", None),
            P(None, "gx", "gy", None),
            P("gx", "gy", None),
            P(),
            P(None, None, "gx", "gy"),
        ),
        check_vma=False,
    )
```

```python
import functools

import jax
import jax.numpy as jnp
from jax import lax
from jax.experimental import pallas as pl
from jax.experimental.pallas import tpu as pltpu
from jax.sharding import PartitionSpec as P

f32 = jnp.float32
bf16 = jnp.bfloat16
MESH = pl.DeviceIdType.MESH

time_step = 0.08
shear_friction_coefficient = 1.5
heat_conduction_coefficient = 1.5

X, Y, Z = 8, 64, 256
XP, YP = 12, 80
STEP_X = 2 * YP
SNAPS = 63
BLOCKS = 48
CHUNK = 32
UNROLL = 8
FAR_LOW = 1
FAR_HIGH = 2
Y_FIRST = True
FACTOR_AT = 1
SPLIT = 4


def flat(ref):
    rows = 1
    for size in ref.shape[:-1]:
        rows *= size
    return ref.reshape(rows, 128)


def split3(value):
    high = value.astype(bf16)
    rest = value - high.astype(f32)
    middle = rest.astype(bf16)
    low = (rest - middle.astype(f32)).astype(bf16)
    return high, middle, low


def z_pair(pair, copied):
    low, high = pair
    lane = lax.broadcasted_iota(jnp.int32, low.shape, 1)
    last, first = lane == 127, lane == 0
    low_up, high_up = pltpu.roll(low, 127, 1), pltpu.roll(high, 127, 1)
    low_down, high_down = pltpu.roll(low, 1, 1), pltpu.roll(high, 1, 1)
    above, below = (high, low) if copied else (0.0, 0.0)
    up = (jnp.where(last, high_up, low_up), jnp.where(last, above, high_up))
    down = (jnp.where(first, below, low_down), jnp.where(first, low_down, high_down))
    return up, down


def primitives(state):
    inverse = 1.0 / state[0]
    return [state[1 + field] * inverse for field in range(4)]


def change(center, x_up, x_down, y_up, y_down, mx_up, mx_down, my_up, my_down, mz):
    up, down = z_pair(mz, False)
    result = [
        [
            (-0.5 * time_step) * ((mx_up[t] - mx_down[t]) + (my_up[t] - my_down[t]) + (up[t] - down[t]))
            for t in range(2)
        ]
    ]
    for field in range(4):
        rate = heat_conduction_coefficient if field == 3 else shear_friction_coefficient
        up, down = z_pair(center[field], field == 3)
        result.append(
            [
                (time_step * rate)
                * (
                    (x_up[field][t] + x_down[field][t])
                    + (y_up[field][t] + y_down[field][t])
                    + (up[t] + down[t])
                    - 6.0 * center[field][t]
                )
                for t in range(2)
            ]
        )
    return result


def change_rows(prim, state, x, row, count):
    def v(dx, dy):
        return [[prim[f, x + dx, t, pl.ds(row + dy, count), :] for t in range(2)] for f in range(4)]

    def s(field, dx, dy):
        return [state[field, x + dx, t, pl.ds(row + dy, count), :] for t in range(2)]

    return change(
        v(0, 0), v(1, 0), v(-1, 0), v(0, 1), v(0, -1),
        s(1, 1, 0), s(1, -1, 0), s(2, 0, 1), s(2, 0, -1), s(3, 0, 0),
    )


def primitive_layer(state, prim, x):
    for row in range(8, 8 + Y, CHUNK):
        for t in range(2):
            values = primitives([state[f, x, t, pl.ds(row, CHUNK), :] for f in range(5)])
            for f in range(4):
                prim[f, x, t, pl.ds(row, CHUNK), :] = values[f]


def first_layer(state, prim, state2, prim2, x):
    for row in range(8, 8 + Y, CHUNK):
        delta = change_rows(prim, state, x, row, CHUNK)
        for t in range(2):
            new = [state[f, x, t, pl.ds(row, CHUNK), :] + delta[f][t] for f in range(5)]
            values = primitives(new)
            for f in range(5):
                state2[f, x, t, pl.ds(row, CHUNK), :] = new[f]
            for f in range(4):
                prim2[f, x, t, pl.ds(row, CHUNK), :] = values[f]


def second_layer(state, state2, prim2, updated, sums, x):
    for row in range(8, 8 + Y, CHUNK):
        delta = change_rows(prim2, state2, x, row, CHUNK)
        for t in range(2):
            new = [
                0.5 * state[f, x, t, pl.ds(row, CHUNK), :]
                + 0.5 * (state2[f, x, t, pl.ds(row, CHUNK), :] + delta[f][t])
                for f in range(5)
            ]
            inverse = 1.0 / new[0]
            for f in range(5):
                updated[f, x - 2, t, pl.ds(row - 8, CHUNK), :] = new[f]
            for c in range(3):
                sums[c, (x - 2) // 4, t, pl.ds(row - 8, CHUNK), :] += new[1 + c] * inverse


def sheet(field, tile, row, dx=0):
    return pl.ds(((field * XP + 2 + dx) * 2 + tile) * YP + row, X, stride=STEP_X)


def place_rows(state, prim, y_in, side):
    row = 7 if side == 0 else 72
    flat_state, flat_prim = flat(state), flat(prim)
    for t in range(2):
        near = [y_in[side, f, 0, t] for f in range(5)]
        values = primitives(near)
        for f in range(4):
            flat_prim[sheet(f, t, row), :] = values[f]
        for f in (1, 2):
            flat_state[sheet(f, t, row), :] = near[f]


def place_corner(state, prim, corner_in, side_x, side_y):
    x = 1 if side_x == 0 else 10
    row = 7 if side_y == 0 else 72
    for t in range(2):
        values = corner_in[side_x, side_y, t]
        inverse = 1.0 / values[0:1]
        for f in range(4):
            prim[f, x, t, pl.ds(row, 1), :] = values[1 + f : 2 + f] * inverse
        for f in (1, 2):
            state[f, x, t, pl.ds(row, 1), :] = values[f : f + 1]


def edge_rows(state, prim, state2, prim2, y_in, side):
    row, own = (7, 8) if side == 0 else (72, 71)
    flat_state, flat_prim = flat(state), flat(prim)
    flat_state2, flat_prim2 = flat(state2), flat(prim2)

    def v(at, dx):
        return [[flat_prim[sheet(f, t, at, dx), :] for t in range(2)] for f in range(4)]

    def s(field, at, dx):
        return [flat_state[sheet(field, t, at, dx), :] for t in range(2)]

    near = [[y_in[side, f, 0, t] for f in range(5)] for t in range(2)]
    far = [primitives([y_in[side, f, 1, t] for f in range(5)]) for t in range(2)]
    far = [[far[t][f] for t in range(2)] for f in range(4)]
    far_my = [y_in[side, 2, 1, t] for t in range(2)]
    inner, inner_my = v(own, 0), s(2, own, 0)
    y_up, y_down, my_up, my_down = (
        (inner, far, inner_my, far_my) if side == 0 else (far, inner, far_my, inner_my)
    )
    delta = change(
        v(row, 0), v(row, 1), v(row, -1), y_up, y_down,
        s(1, row, 1), s(1, row, -1), my_up, my_down, [near[t][3] for t in range(2)],
    )
    for t in range(2):
        new = [near[t][f] + delta[f][t] for f in range(5)]
        values = primitives(new)
        for f in range(4):
            flat_prim2[sheet(f, t, row), :] = values[f]
        flat_state2[sheet(2, t, row), :] = new[2]


def eliminate(rows, first, stop):
    sub = lax.broadcasted_iota(jnp.int32, (8, 128), 0)
    for block in range(first, stop):
        columns = [
            [jnp.broadcast_to(rows[b][:, 8 * block + j : 8 * block + j + 1], (8, 128)) for b in range(block, 8)]
            for j in range(8)
        ]
        corner = {
            (i, j): jnp.broadcast_to(columns[j][0][i : i + 1, :], (8, 128)) for j in range(8) for i in range(j, 8)
        }
        pivot_rows = [jnp.broadcast_to(rows[block][i : i + 1, :], (8, 128)) for i in range(8)]
        for j in range(8):
            inverse = 1.0 / corner[j, j]
            ratio = {i: corner[i, j] * inverse for i in range(j + 1, 8)}
            for i in range(j + 1, 8):
                for n in range(j + 1, i + 1):
                    corner[i, n] = corner[i, n] - ratio[i] * corner[n, j]
                pivot_rows[i] = pivot_rows[i] - ratio[i] * pivot_rows[j]
                for b in range(8 - block):
                    columns[i][b] = columns[i][b] - ratio[i] * columns[j][b]
            scaled = pivot_rows[j] * inverse
            for b in range(8 - block):
                column = jnp.where(sub > j, columns[j][b], 0.0) if b == 0 else columns[j][b]
                rows[block + b] = rows[block + b] - column * scaled
    return rows


def kernel(
    rows_all, sizes,
    density, momentum, energy, snapshots,
    out_density, out_momentum, out_energy, out_factor, out_modes,
    state, prim, state2, prim2, updated, sums,
    y_out, y_in, corner_out, corner_in,
    snap_in, snap_f, snap_b, modes, factor_v, lower_v, coarse,
    gram, gram_part, gram_z, gram_y, gram_all, gram_sums,
    dot_gy, dot_z, dot_y, dot_sums,
    load_sem, store_sem,
    x_send, x_recv, y_send, y_recv, corner_send, corner_recv,
    gram_send, gram_recv, dot_send, dot_recv,
):
    n_gx, n_gy, n_y = sizes
    n_z = n_gx // n_y
    gx, gy = lax.axis_index("gx"), lax.axis_index("gy")
    iz, iy = lax.div(gx, n_y), lax.rem(gx, n_y)

    def moved(dx, dy):
        return {"gx": lax.rem(gx + dx + n_gx, n_gx), "gy": lax.rem(gy + dy + n_gy, n_gy)}

    def on_gy(i):
        return {"gx": gx, "gy": i}

    def on_z(i):
        return {"gx": i * n_y + iy, "gy": gy}

    def on_y(i):
        return {"gx": iz * n_y + i, "gy": gy}

    loads = []
    for t in range(2):
        lanes, rows = pl.ds(128 * t, 128), pl.ds(8, Y)
        loads += [
            pltpu.make_async_copy(density.at[:, :, lanes], state.at[0, pl.ds(2, X), t, rows, :], load_sem.at[3 * t]),
            pltpu.make_async_copy(
                momentum.at[:, :, :, lanes], state.at[pl.ds(1, 3), pl.ds(2, X), t, rows, :], load_sem.at[3 * t + 1]
            ),
            pltpu.make_async_copy(energy.at[:, :, lanes], state.at[4, pl.ds(2, X), t, rows, :], load_sem.at[3 * t + 2]),
        ]
    load_snapshots = pltpu.make_async_copy(snapshots, snap_in, load_sem.at[6])
    for copy in loads:
        copy.start()
    load_snapshots.start()

    barrier = pltpu.get_barrier_semaphore()
    greeted = [moved(dx, dy) for dx in (-1, 1) for dy in (-1, 0, 1)]
    greeted += [on_gy(lax.rem(gy + d, n_gy)) for d in range(1, n_gy)]
    greeted += [on_z(lax.rem(iz + d, n_z)) for d in range(1, n_z)]
    greeted += [on_y(lax.rem(iy + d, n_y)) for d in range(1, n_y)]
    for device in greeted:
        pl.semaphore_signal(barrier, inc=1, device_id=device, device_id_type=MESH)
    pl.semaphore_wait(barrier, len(greeted))

    def remote(source, target, send_sem, recv_sem, device):
        return pltpu.make_async_remote_copy(
            src_ref=source, dst_ref=target, send_sem=send_sem, recv_sem=recv_sem, device_id=device, device_id_type=MESH
        )

    def x_copies(layer):
        copies = []
        for side in range(2):
            source, target = (X - 1 - layer, 1 - layer) if side == 0 else (layer, 10 + layer)
            device = moved(1, 0) if side == 0 else moved(-1, 0)
            for t in range(2):
                lanes, rows = pl.ds(128 * t, 128), pl.ds(8, Y)
                at = ((layer * 2 + side) * 2 + t) * 3
                copies += [
                    remote(
                        density.at[source, :, lanes], state.at[0, target, t, rows, :],
                        x_send.at[at], x_recv.at[at], device,
                    ),
                    remote(
                        momentum.at[:, source, :, lanes], state.at[pl.ds(1, 3), target, t, rows, :],
                        x_send.at[at + 1], x_recv.at[at + 1], device,
                    ),
                    remote(
                        energy.at[source, :, lanes], state.at[4, target, t, rows, :],
                        x_send.at[at + 2], x_recv.at[at + 2], device,
                    ),
                ]
        return copies

    def start(copies):
        for copy in copies:
            copy.start()

    def wait(copies):
        for copy in copies:
            copy.wait()

    def loop(first, stop, step):
        lax.fori_loop(first, stop, lambda x, _: (step(x), 0)[1], 0)

    def exchange(sources, target, me, count, device_of, send, recv, first):
        copies = []
        for d in sorted(range(1, count), key=lambda d: -min(d, count - d)):
            peer = lax.rem(me + d, count)
            copies.append(
                remote(sources(peer), target.at[me], send.at[first + d], recv.at[first + d], device_of(peer))
            )
        start(copies)
        return copies

    def total(ref, count):
        value = ref[0]
        for i in range(1, count):
            value = value + ref[i]
        return value

    near_copies, far_copies = x_copies(0), x_copies(1)

    def start_far(point):
        for t, chosen in enumerate((FAR_LOW, FAR_HIGH)):
            if chosen == point:
                start(far_copies[3 * t : 3 * t + 3] + far_copies[6 + 3 * t : 9 + 3 * t])

    along_z, along_y = (gram_z, iz, n_z, on_z), (gram_y, iy, n_y, on_y)
    second, third = (along_y, along_z) if Y_FIRST else (along_z, along_y)

    def gram_stage(stage, value):
        target, me, count, device_of = (second, third)[stage]
        gram_sums[stage] = value
        copies = exchange(lambda peer: gram_sums.at[stage], target, me, count, device_of, gram_send, gram_recv, 8 + 8 * stage)
        target[me] = value
        return copies

    start(near_copies)

    load_snapshots.wait()
    for c in range(3):
        snap_f[0:SNAPS, c] = snap_in[:, c].astype(f32)
    snap_f[SNAPS] = jnp.zeros((3, 16, 128), f32)
    flat_snap, flat_modes = flat(snap_f), flat(modes)

    def gram_step(i, value):
        for part in range(UNROLL):
            at = UNROLL * i + part
            pair = [flat_snap[pl.ds(2 * at + half, 64, stride=BLOCKS), :] for half in range(2)]
            pair = jnp.concatenate(pair, axis=1).astype(bf16)
            snap_b[at] = pair
            value = value + lax.dot_general(pair, pair, (((1,), (1,)), ((), ())), preferred_element_type=f32)
        return value

    local = lax.fori_loop(0, BLOCKS // 2 // UNROLL, gram_step, jnp.zeros((64, 64), f32))
    local = jnp.concatenate([local, jnp.zeros((64, 64), f32)], axis=1)
    for b in range(8):
        gram[b] = local[8 * b : 8 * b + 8]
    scatter = exchange(lambda peer: gram.at[peer], gram_part, gy, n_gy, on_gy, gram_send, gram_recv, 0)
    gram_part[gy] = gram[gy]

    wait(loads)
    flat_state = flat(state)
    for side in range(2):
        for f in range(5):
            for far in range(2):
                y = Y - 1 - far if side == 0 else far
                for t in range(2):
                    y_out[side, f, far, t] = flat_state[sheet(f, t, 8 + y), :]
    y_copies = [
        remote(y_out.at[side], y_in.at[side], y_send.at[side], y_recv.at[side], moved(0, 1 - 2 * side))
        for side in range(2)
    ]
    start(y_copies)
    corner_out[...] = jnp.zeros_like(corner_out)
    corner_copies = []
    for side_x in range(2):
        for side_y in range(2):
            x, y = (X - 1) * (1 - side_x), (Y - 1) * (1 - side_y)
            for t in range(2):
                begin = ((2 + x) * 2 + t) * YP + 8 + y
                corner_out[side_x, side_y, t, 0:5] = flat_state[pl.ds(begin, 5, stride=XP * STEP_X), :]
            at = side_x * 2 + side_y
            corner_copies.append(
                remote(
                    corner_out.at[side_x, side_y], corner_in.at[side_x, side_y],
                    corner_send.at[at], corner_recv.at[at], moved(1 - 2 * side_x, 1 - 2 * side_y),
                )
            )
    start(corner_copies)
    start_far(0)

    loop(2, 2 + X, lambda x: primitive_layer(state, prim, x))
    wait(scatter)
    copies = gram_stage(0, total(gram_part, n_gy))
    start_far(1)
    wait(y_copies)
    for side in range(2):
        place_rows(state, prim, y_in, side)
    loop(3, 1 + X, lambda x: first_layer(state, prim, state2, prim2, x))
    sums[...] = jnp.zeros_like(sums)
    wait(copies)
    copies = gram_stage(1, total(second[0], second[2]))
    start_far(2)
    wait(near_copies + corner_copies)
    loop(0, 2, lambda i: primitive_layer(state, prim, 1 + 9 * i))
    for side_x in range(2):
        for side_y in range(2):
            place_corner(state, prim, corner_in, side_x, side_y)
    loop(0, 2, lambda i: first_layer(state, prim, state2, prim2, 2 + 7 * i))
    for side in range(2):
        edge_rows(state, prim, state2, prim2, y_in, side)
    wait(copies)
    gram_sums[2] = total(third[0], third[2])
    gather = exchange(lambda peer: gram_sums.at[2], gram_all, gy, n_gy, on_gy, gram_send, gram_recv, 24)
    gram_all[gy] = gram_sums[2]
    loop(3, 1 + X, lambda x: second_layer(state, state2, prim2, updated, sums, x))
    lane = lax.broadcasted_iota(jnp.int32, (8, 128), 1)
    sub = lax.broadcasted_iota(jnp.int32, (8, 128), 0)

    def factor_start():
        wait(gather)
        blocks = []
        for b in range(8):
            row = sub + 8 * b
            known = (row < SNAPS) & (lane < SNAPS)
            unit = ((lane == row) & (row == SNAPS)) | (lane == row + 64)
            blocks.append(jnp.where(known, gram_all[b] / rows_all, jnp.where(unit, 1.0, 0.0)))
        return eliminate(blocks, 0, SPLIT)

    if FACTOR_AT == 2:
        blocks = factor_start()
    wait(far_copies)
    loop(0, 2, lambda i: primitive_layer(state, prim, 11 * i))
    loop(0, 2, lambda i: first_layer(state, prim, state2, prim2, 1 + 9 * i))
    loop(0, 2, lambda i: second_layer(state, state2, prim2, updated, sums, 2 + 7 * i))

    flat_sums = flat(sums)
    columns = []
    for half in range(2):
        for t in range(2):
            parts = []
            for c in range(6):
                begin = (c * 2 + t) * Y + 4 * half
                part = flat_sums[pl.ds(begin, 8, stride=8), :]
                for k in range(1, 4):
                    part = part + flat_sums[pl.ds(begin + k, 8, stride=8), :]
                parts.append(part)
            columns.append(jnp.concatenate(parts, axis=0))
    fine = jnp.concatenate(columns, axis=1)
    source = lax.broadcasted_iota(jnp.int32, (512, 128), 0)
    target = lax.broadcasted_iota(jnp.int32, (512, 128), 1)
    selection = jnp.where(lax.shift_right_logical(source, 2) == target, 1.0 / 64.0, 0.0).astype(bf16)
    means = sum(jnp.dot(part, selection, preferred_element_type=f32) for part in split3(fine))
    for c in range(3):
        for half in range(2):
            at = (2 * c + half) * 8
            coarse[pl.ds(16 * c + half, 8, stride=2), :] = means[at : at + 8]

    def dot_step(i, acc):
        for part in range(4):
            b = 4 * i + part
            acc = acc + flat_snap[pl.ds(b, 64, stride=BLOCKS), :] * coarse[pl.ds(b, 1), :]
        return acc

    acc = lax.fori_loop(0, BLOCKS // 4, dot_step, jnp.zeros((64, 128), f32))
    squares = jnp.sum(coarse[...] * coarse[...], axis=0, keepdims=True)
    acc = jnp.where(lax.broadcasted_iota(jnp.int32, (64, 128), 0) == SNAPS, squares, acc)
    ones = jnp.ones((8, 128), bf16)
    products = sum(
        lax.dot_general(ones, part, (((1,), (1,)), ((), ())), preferred_element_type=f32) for part in split3(acc)
    )
    dot_sums[0] = jnp.concatenate([products, jnp.zeros((8, 64), f32)], axis=1)
    copies = exchange(lambda peer: dot_sums.at[0], dot_gy, gy, n_gy, on_gy, dot_send, dot_recv, 0)
    dot_gy[gy] = dot_sums[0]

    stores = []
    for t in range(2):
        lanes = pl.ds(128 * t, 128)
        stores += [
            pltpu.make_async_copy(updated.at[0, :, t], out_density.at[:, :, lanes], store_sem.at[3 * t]),
            pltpu.make_async_copy(updated.at[pl.ds(1, 3), :, t], out_momentum.at[:, :, :, lanes], store_sem.at[3 * t + 1]),
            pltpu.make_async_copy(updated.at[4, :, t], out_energy.at[:, :, lanes], store_sem.at[3 * t + 2]),
        ]
    start(stores)
    if FACTOR_AT == 0:
        blocks = factor_start()
    wait(copies)
    dot_sums[1] = total(dot_gy, n_gy)
    copies = exchange(lambda peer: dot_sums.at[1], dot_z, iz, n_z, on_z, dot_send, dot_recv, 8)
    dot_z[iz] = dot_sums[1]
    if FACTOR_AT == 1:
        blocks = factor_start()
    blocks = eliminate(blocks, SPLIT, 8)
    for b in range(8):
        row = sub + 8 * b
        diagonal = jnp.sum(jnp.where(lane == row, blocks[b], 0.0), axis=1, keepdims=True)
        scaled = blocks[b] * (1.0 / jnp.sqrt(diagonal))
        factor_v[b] = jnp.where((lane >= row) & (lane < SNAPS), scaled, 0.0)
        lower_v[b] = jnp.where((row < SNAPS) & (lane < 64), pltpu.roll(scaled, 64, 1), 0.0)
    wait(copies)
    dot_sums[2] = total(dot_z, n_z)
    copies = exchange(lambda peer: dot_sums.at[2], dot_y, iy, n_y, on_y, dot_send, dot_recv, 16)
    dot_y[iy] = dot_sums[2]
    stacked = jnp.concatenate(split3(lower_v[...].reshape(64, 128)[:, :64]), axis=0)

    def modes_step(i, carry):
        for part in range(BLOCKS // 2):
            at = BLOCKS // 2 * i + part
            parts = jnp.dot(stacked, snap_b[at], preferred_element_type=f32)
            both = parts[0:64] + (parts[64:128] + parts[128:192])
            for half in range(2):
                flat_modes[pl.ds(2 * at + half, 64, stride=BLOCKS), :] = both[:, 128 * half : 128 * half + 128]
        return carry

    lax.fori_loop(0, 1, modes_step, 0)
    store_modes = pltpu.make_async_copy(
        flat_modes.at[pl.ds(0, SNAPS * BLOCKS)], out_modes.at[pl.ds(0, SNAPS * BLOCKS)], store_sem.at[6]
    )
    store_modes.start()
    wait(copies)
    share = total(dot_y, n_y) / rows_all

    own = jnp.where(lane < SNAPS, share, 0.0)
    left = jnp.sum(jnp.where(lane == SNAPS, share, 0.0), axis=1, keepdims=True)[0:1]
    weights = []
    for b in range(8):
        weights.append(jnp.sum(lower_v[b] * own, axis=1, keepdims=True))
        left = left - jnp.sum(weights[b] * weights[b], axis=0, keepdims=True)
    last = jnp.broadcast_to(jnp.sqrt(left), (8, 128))
    mode = [coarse[8 * i : 8 * i + 8, :] for i in range(6)]
    for b in range(8):
        row = sub + 8 * b
        weight = jnp.broadcast_to(weights[b], (8, 128))
        column = jnp.where(row == SNAPS, last, weight)
        out_factor[8 * b : 8 * b + 8, :] = jnp.where(lane == SNAPS, column, factor_v[b])[:, :64]
        for at in range(8 if b < 7 else 7):
            one = jnp.broadcast_to(weight[at : at + 1], (8, 128))
            begin = BLOCKS * (8 * b + at)
            for i in range(6):
                mode[i] = mode[i] - one * flat_modes[begin + 8 * i : begin + 8 * i + 8, :]
    scale = 1.0 / last
    for i in range(6):
        flat_modes[BLOCKS * SNAPS + 8 * i : BLOCKS * SNAPS + 8 * i + 8, :] = mode[i] * scale
    store_last = pltpu.make_async_copy(
        flat_modes.at[pl.ds(SNAPS * BLOCKS, BLOCKS)], out_modes.at[pl.ds(SNAPS * BLOCKS, BLOCKS)], store_sem.at[7]
    )
    store_last.start()
    wait(stores + [store_modes, store_last])


def copy_out(*refs):
    sources, targets, sem = refs[:5], refs[5:10], refs[10]
    copies = []

    def add(source, target):
        copies.append(pltpu.make_async_copy(source, target, sem.at[len(copies)]))

    for source, target in zip(sources, targets):
        if source.ndim == 4:
            for c in range(source.shape[0]):
                for half in range(2):
                    part = pl.ds(source.shape[1] // 2 * half, source.shape[1] // 2)
                    add(source.at[c, part], target.at[c, part])
        elif source.shape[0] == 64:
            add(source, target)
        else:
            pieces = 2 if source.ndim == 3 else 6
            size = source.shape[0] // pieces
            for piece in range(pieces):
                part = pl.ds(size * piece, size)
                add(source.at[part], target.at[part])
    for copy in copies:
        copy.start()
    for copy in copies:
        copy.wait()


def solution(mesh):
    n_gx, n_gy = mesh.shape["gx"], mesh.shape["gy"]
    n_y = 4
    n_z = n_gx // n_y

    def on_device(density, momentum, energy, snapshots):
        rows_all = 6144 * n_gx * n_gy
        snapshots = snapshots.reshape(SNAPS, 3, 2, 8, 128).transpose(0, 1, 3, 2, 4).reshape(SNAPS, 3, 16, 128)
        anywhere = pl.BlockSpec(memory_space=pl.ANY)
        vmem = pl.BlockSpec(memory_space=pltpu.VMEM)
        dma = pltpu.SemaphoreType.DMA
        results = pl.pallas_call(
            functools.partial(kernel, float(rows_all), (n_gx, n_gy, n_y)),
            name="sections_and_modes",
            in_specs=[pl.BlockSpec(memory_space=pltpu.HBM)] * 4,
            out_specs=(anywhere, anywhere, anywhere, vmem, anywhere),
            out_shape=(
                jax.ShapeDtypeStruct((X, Y, Z), f32),
                jax.ShapeDtypeStruct((3, X, Y, Z), f32),
                jax.ShapeDtypeStruct((X, Y, Z), f32),
                jax.ShapeDtypeStruct((64, 64), f32),
                jax.ShapeDtypeStruct((64 * BLOCKS, 128), f32),
            ),
            scratch_shapes=[
                pltpu.VMEM((5, XP, 2, YP, 128), f32),
                pltpu.VMEM((4, XP, 2, YP, 128), f32),
                pltpu.VMEM((5, XP, 2, YP, 128), f32),
                pltpu.VMEM((4, XP, 2, YP, 128), f32),
                pltpu.VMEM((5, X, 2, Y, 128), f32),
                pltpu.VMEM((3, 2, 2, Y, 128), f32),
                pltpu.VMEM((2, 5, 2, 2, 8, 128), f32),
                pltpu.VMEM((2, 5, 2, 2, 8, 128), f32),
                pltpu.VMEM((2, 2, 2, 8, 128), f32),
                pltpu.VMEM((2, 2, 2, 8, 128), f32),
                pltpu.VMEM((SNAPS, 3, 16, 128), bf16),
                pltpu.VMEM((64, 3, 16, 128), f32),
                pltpu.VMEM((BLOCKS // 2, 64, 256), bf16),
                pltpu.VMEM((64, 3, 16, 128), f32),
                pltpu.VMEM((8, 8, 128), f32),
                pltpu.VMEM((8, 8, 128), f32),
                pltpu.VMEM((BLOCKS, 128), f32),
                pltpu.VMEM((8, 8, 128), f32),
                pltpu.VMEM((n_gy, 8, 128), f32),
                pltpu.VMEM((n_z, 8, 128), f32),
                pltpu.VMEM((n_y, 8, 128), f32),
                pltpu.VMEM((8, 8, 128), f32),
                pltpu.VMEM((3, 8, 128), f32),
                pltpu.VMEM((n_gy, 8, 128), f32),
                pltpu.VMEM((n_z, 8, 128), f32),
                pltpu.VMEM((n_y, 8, 128), f32),
                pltpu.VMEM((4, 8, 128), f32),
                dma((7,)),
                dma((8,)),
                dma((24,)),
                dma((24,)),
                dma((2,)),
                dma((2,)),
                dma((4,)),
                dma((4,)),
                dma((32,)),
                dma((32,)),
                dma((24,)),
                dma((24,)),
            ],
            compiler_params=pltpu.CompilerParams(
                collective_id=0, has_side_effects=True, vmem_limit_bytes=32 * 2**20
            ),
        )(*(pltpu.with_memory_space_constraint(a, pltpu.HBM) for a in (density, momentum, energy, snapshots)))
        new_density, new_momentum, new_energy, factor, modes = pl.pallas_call(
            copy_out,
            name="copy_out",
            in_specs=[anywhere] * 5,
            out_specs=[pl.BlockSpec(memory_space=pltpu.HBM)] * 5,
            out_shape=[jax.ShapeDtypeStruct(value.shape, f32) for value in results],
            scratch_shapes=[dma((17,))],
            compiler_params=pltpu.CompilerParams(vmem_limit_bytes=2**20),
        )(*results)
        modes = modes.reshape(64, 3, 8, 2, 128).transpose(0, 1, 3, 2, 4).reshape(64, 3, 2, 1024)
        return new_density, new_momentum, new_energy, factor, modes

    placed = (
        P("gx", "gy", None),
        P(None, "gx", "gy", None),
        P("gx", "gy", None),
        P(None, None, "gx", "gy"),
    )
    return jax.shard_map(
        on_device,
        mesh=mesh,
        in_specs=placed,
        out_specs=(
            P("gx", "gy", None),
            P(None, "gx", "gy", None),
            P("gx", "gy", None),
            P(),
            P(None, None, "gx", "gy"),
        ),
        check_vma=False,
    )
```

```python
import functools

import jax
import jax.numpy as jnp
from jax import lax
from jax.experimental import pallas as pl
from jax.experimental.pallas import tpu as pltpu
from jax.sharding import PartitionSpec as P

f32 = jnp.float32
bf16 = jnp.bfloat16
MESH = pl.DeviceIdType.MESH

time_step = 0.08
shear_friction_coefficient = 1.5
heat_conduction_coefficient = 1.5

X, Y, Z = 8, 64, 256
XP, YP = 12, 80
STEP_X = 2 * YP
SNAPS = 63
BLOCKS = 48
CHUNK = 32
UNROLL = 8
FAR_LOW = 1
FAR_HIGH = 2
Y_FIRST = True
FACTOR_AT = 1
SPLIT = 4


def flat(ref):
    rows = 1
    for size in ref.shape[:-1]:
        rows *= size
    return ref.reshape(rows, 128)


def split3(value):
    high = value.astype(bf16)
    rest = value - high.astype(f32)
    middle = rest.astype(bf16)
    low = (rest - middle.astype(f32)).astype(bf16)
    return high, middle, low


def z_pair(pair, copied):
    low, high = pair
    lane = lax.broadcasted_iota(jnp.int32, low.shape, 1)
    last, first = lane == 127, lane == 0
    low_up, high_up = pltpu.roll(low, 127, 1), pltpu.roll(high, 127, 1)
    low_down, high_down = pltpu.roll(low, 1, 1), pltpu.roll(high, 1, 1)
    above, below = (high, low) if copied else (0.0, 0.0)
    up = (jnp.where(last, high_up, low_up), jnp.where(last, above, high_up))
    down = (jnp.where(first, below, low_down), jnp.where(first, low_down, high_down))
    return up, down


def primitives(state):
    inverse = 1.0 / state[0]
    return [state[1 + field] * inverse for field in range(4)]


def change(center, x_up, x_down, y_up, y_down, mx_up, mx_down, my_up, my_down, mz):
    up, down = z_pair(mz, False)
    result = [
        [
            (-0.5 * time_step) * ((mx_up[t] - mx_down[t]) + (my_up[t] - my_down[t]) + (up[t] - down[t]))
            for t in range(2)
        ]
    ]
    for field in range(4):
        rate = heat_conduction_coefficient if field == 3 else shear_friction_coefficient
        up, down = z_pair(center[field], field == 3)
        result.append(
            [
                (time_step * rate)
                * (
                    (x_up[field][t] + x_down[field][t])
                    + (y_up[field][t] + y_down[field][t])
                    + (up[t] + down[t])
                    - 6.0 * center[field][t]
                )
                for t in range(2)
            ]
        )
    return result


def change_rows(prim, state, x, row, count):
    def v(dx, dy):
        return [[prim[f, x + dx, t, pl.ds(row + dy, count), :] for t in range(2)] for f in range(4)]

    def s(field, dx, dy):
        return [state[field, x + dx, t, pl.ds(row + dy, count), :] for t in range(2)]

    return change(
        v(0, 0), v(1, 0), v(-1, 0), v(0, 1), v(0, -1),
        s(1, 1, 0), s(1, -1, 0), s(2, 0, 1), s(2, 0, -1), s(3, 0, 0),
    )


def primitive_layer(state, prim, x, begin=0, end=Y):
    for row in range(8 + begin, 8 + end, CHUNK):
        for t in range(2):
            values = primitives([state[f, x, t, pl.ds(row, CHUNK), :] for f in range(5)])
            for f in range(4):
                prim[f, x, t, pl.ds(row, CHUNK), :] = values[f]


def first_layer(state, prim, state2, prim2, x, begin=0, end=Y):
    for row in range(8 + begin, 8 + end, CHUNK):
        delta = change_rows(prim, state, x, row, CHUNK)
        for t in range(2):
            new = [state[f, x, t, pl.ds(row, CHUNK), :] + delta[f][t] for f in range(5)]
            values = primitives(new)
            for f in range(5):
                state2[f, x, t, pl.ds(row, CHUNK), :] = new[f]
            for f in range(4):
                prim2[f, x, t, pl.ds(row, CHUNK), :] = values[f]


def second_layer(state, state2, prim2, updated, sums, x, begin=0, end=Y):
    for row in range(8 + begin, 8 + end, CHUNK):
        delta = change_rows(prim2, state2, x, row, CHUNK)
        for t in range(2):
            new = [
                0.5 * state[f, x, t, pl.ds(row, CHUNK), :]
                + 0.5 * (state2[f, x, t, pl.ds(row, CHUNK), :] + delta[f][t])
                for f in range(5)
            ]
            inverse = 1.0 / new[0]
            for f in range(5):
                updated[f, x - 2, t, pl.ds(row - 8, CHUNK), :] = new[f]
            for c in range(3):
                sums[c, (x - 2) // 4, t, pl.ds(row - 8, CHUNK), :] += new[1 + c] * inverse


def sheet(field, tile, row, dx=0):
    return pl.ds(((field * XP + 2 + dx) * 2 + tile) * YP + row, X, stride=STEP_X)


def place_rows(state, prim, y_in, side):
    row = 7 if side == 0 else 72
    flat_state, flat_prim = flat(state), flat(prim)
    for t in range(2):
        near = [y_in[side, f, 0, t] for f in range(5)]
        values = primitives(near)
        for f in range(4):
            flat_prim[sheet(f, t, row), :] = values[f]
        for f in (1, 2):
            flat_state[sheet(f, t, row), :] = near[f]


def place_corner(state, prim, corner_in, side_x, side_y):
    x = 1 if side_x == 0 else 10
    row = 7 if side_y == 0 else 72
    for t in range(2):
        values = corner_in[side_x, side_y, t]
        inverse = 1.0 / values[0:1]
        for f in range(4):
            prim[f, x, t, pl.ds(row, 1), :] = values[1 + f : 2 + f] * inverse
        for f in (1, 2):
            state[f, x, t, pl.ds(row, 1), :] = values[f : f + 1]


def edge_rows(state, prim, state2, prim2, y_in, side):
    row, own = (7, 8) if side == 0 else (72, 71)
    flat_state, flat_prim = flat(state), flat(prim)
    flat_state2, flat_prim2 = flat(state2), flat(prim2)

    def v(at, dx):
        return [[flat_prim[sheet(f, t, at, dx), :] for t in range(2)] for f in range(4)]

    def s(field, at, dx):
        return [flat_state[sheet(field, t, at, dx), :] for t in range(2)]

    near = [[y_in[side, f, 0, t] for f in range(5)] for t in range(2)]
    far = [primitives([y_in[side, f, 1, t] for f in range(5)]) for t in range(2)]
    far = [[far[t][f] for t in range(2)] for f in range(4)]
    far_my = [y_in[side, 2, 1, t] for t in range(2)]
    inner, inner_my = v(own, 0), s(2, own, 0)
    y_up, y_down, my_up, my_down = (
        (inner, far, inner_my, far_my) if side == 0 else (far, inner, far_my, inner_my)
    )
    delta = change(
        v(row, 0), v(row, 1), v(row, -1), y_up, y_down,
        s(1, row, 1), s(1, row, -1), my_up, my_down, [near[t][3] for t in range(2)],
    )
    for t in range(2):
        new = [near[t][f] + delta[f][t] for f in range(5)]
        values = primitives(new)
        for f in range(4):
            flat_prim2[sheet(f, t, row), :] = values[f]
        flat_state2[sheet(2, t, row), :] = new[2]


def eliminate(rows, first, stop):
    sub = lax.broadcasted_iota(jnp.int32, (8, 128), 0)
    for block in range(first, stop):
        columns = [
            [jnp.broadcast_to(rows[b][:, 8 * block + j : 8 * block + j + 1], (8, 128)) for b in range(block, 8)]
            for j in range(8)
        ]
        corner = {
            (i, j): jnp.broadcast_to(columns[j][0][i : i + 1, :], (8, 128)) for j in range(8) for i in range(j, 8)
        }
        pivot_rows = [jnp.broadcast_to(rows[block][i : i + 1, :], (8, 128)) for i in range(8)]
        for j in range(8):
            inverse = 1.0 / corner[j, j]
            ratio = {i: corner[i, j] * inverse for i in range(j + 1, 8)}
            for i in range(j + 1, 8):
                for n in range(j + 1, i + 1):
                    corner[i, n] = corner[i, n] - ratio[i] * corner[n, j]
                pivot_rows[i] = pivot_rows[i] - ratio[i] * pivot_rows[j]
                for b in range(8 - block):
                    columns[i][b] = columns[i][b] - ratio[i] * columns[j][b]
            scaled = pivot_rows[j] * inverse
            for b in range(8 - block):
                column = jnp.where(sub > j, columns[j][b], 0.0) if b == 0 else columns[j][b]
                rows[block + b] = rows[block + b] - column * scaled
    return rows


def kernel(
    rows_all, sizes,
    density, momentum, energy, snapshots,
    out_density, out_momentum, out_energy, out_factor, out_modes, out_last,
    state, prim, state2, prim2, updated, sums,
    y_out, y_in, corner_out, corner_in,
    snap_in, snap_f, snap_b, modes, factor_v, lower_v, coarse,
    gram, gram_part, gram_z, gram_y, gram_all, gram_sums,
    dot_gy, dot_z, dot_y, dot_sums,
    load_sem, store_sem,
    x_send, x_recv, y_send, y_recv, corner_send, corner_recv,
    gram_send, gram_recv, dot_send, dot_recv,
):
    n_gx, n_gy, n_y = sizes
    n_z = n_gx // n_y
    gx, gy = lax.axis_index("gx"), lax.axis_index("gy")
    iz, iy = lax.div(gx, n_y), lax.rem(gx, n_y)

    def moved(dx, dy):
        return {"gx": lax.rem(gx + dx + n_gx, n_gx), "gy": lax.rem(gy + dy + n_gy, n_gy)}

    def on_gy(i):
        return {"gx": gx, "gy": i}

    def on_z(i):
        return {"gx": i * n_y + iy, "gy": gy}

    def on_y(i):
        return {"gx": iz * n_y + i, "gy": gy}

    loads = []
    for t in range(2):
        lanes, rows = pl.ds(128 * t, 128), pl.ds(8, Y)
        loads += [
            pltpu.make_async_copy(density.at[:, :, lanes], state.at[0, pl.ds(2, X), t, rows, :], load_sem.at[3 * t]),
            pltpu.make_async_copy(
                momentum.at[:, :, :, lanes], state.at[pl.ds(1, 3), pl.ds(2, X), t, rows, :], load_sem.at[3 * t + 1]
            ),
            pltpu.make_async_copy(energy.at[:, :, lanes], state.at[4, pl.ds(2, X), t, rows, :], load_sem.at[3 * t + 2]),
        ]
    load_snapshots = pltpu.make_async_copy(snapshots, snap_in, load_sem.at[6])
    for copy in loads:
        copy.start()
    load_snapshots.start()

    barrier = pltpu.get_barrier_semaphore()
    greeted = [moved(dx, dy) for dx in (-1, 1) for dy in (-1, 0, 1)]
    greeted += [on_gy(lax.rem(gy + d, n_gy)) for d in range(1, n_gy)]
    greeted += [on_z(lax.rem(iz + d, n_z)) for d in range(1, n_z)]
    greeted += [on_y(lax.rem(iy + d, n_y)) for d in range(1, n_y)]
    for device in greeted:
        pl.semaphore_signal(barrier, inc=1, device_id=device, device_id_type=MESH)
    pl.semaphore_wait(barrier, len(greeted))

    def remote(source, target, send_sem, recv_sem, device):
        return pltpu.make_async_remote_copy(
            src_ref=source, dst_ref=target, send_sem=send_sem, recv_sem=recv_sem, device_id=device, device_id_type=MESH
        )

    def x_copies(layer, begin, count, at):
        copies = []
        for side in range(2):
            source, target = (X - 1 - layer, 1 - layer) if side == 0 else (layer, 10 + layer)
            device = moved(1, 0) if side == 0 else moved(-1, 0)
            own, rows = pl.ds(begin, count), pl.ds(8 + begin, count)
            for t in range(2):
                lanes = pl.ds(128 * t, 128)
                copies += [
                    remote(
                        density.at[source, own, lanes], state.at[0, target, t, rows, :],
                        x_send.at[at], x_recv.at[at], device,
                    ),
                    remote(
                        momentum.at[:, source, own, lanes], state.at[pl.ds(1, 3), target, t, rows, :],
                        x_send.at[at + 1], x_recv.at[at + 1], device,
                    ),
                    remote(
                        energy.at[source, own, lanes], state.at[4, target, t, rows, :],
                        x_send.at[at + 2], x_recv.at[at + 2], device,
                    ),
                ]
                at += 3
        return copies

    def start(copies):
        for copy in copies:
            copy.start()

    def wait(copies):
        for copy in copies:
            copy.wait()

    def loop(first, stop, step):
        lax.fori_loop(first, stop, lambda x, _: (step(x), 0)[1], 0)

    def exchange(sources, target, me, count, device_of, send, recv, first):
        copies = []
        for d in sorted(range(1, count), key=lambda d: -min(d, count - d)):
            peer = lax.rem(me + d, count)
            copies.append(
                remote(sources(peer), target.at[me], send.at[first + d], recv.at[first + d], device_of(peer))
            )
        start(copies)
        return copies

    def total(ref, count):
        value = ref[0]
        for i in range(1, count):
            value = value + ref[i]
        return value

    near_copies = x_copies(0, 0, Y, 0)
    far_copies = [x_copies(1, CHUNK * half, CHUNK, 12 + 12 * half) for half in range(2)]

    def start_far(point):
        for half, chosen in enumerate((FAR_LOW, FAR_HIGH)):
            if chosen == point:
                start(far_copies[half])

    along_z, along_y = (gram_z, iz, n_z, on_z), (gram_y, iy, n_y, on_y)
    second, third = (along_y, along_z) if Y_FIRST else (along_z, along_y)

    def gram_stage(stage, value):
        target, me, count, device_of = (second, third)[stage]
        gram_sums[stage] = value
        copies = exchange(lambda peer: gram_sums.at[stage], target, me, count, device_of, gram_send, gram_recv, 8 + 8 * stage)
        target[me] = value
        return copies

    start(near_copies)

    load_snapshots.wait()
    for c in range(3):
        snap_f[0:SNAPS, c] = snap_in[:, c].astype(f32)
    snap_f[SNAPS] = jnp.zeros((3, 16, 128), f32)
    flat_snap, flat_modes = flat(snap_f), flat(modes)

    def gram_step(i, value):
        for part in range(UNROLL):
            at = UNROLL * i + part
            pair = [flat_snap[pl.ds(2 * at + half, 64, stride=BLOCKS), :] for half in range(2)]
            pair = jnp.concatenate(pair, axis=1).astype(bf16)
            snap_b[at] = pair
            value = value + lax.dot_general(pair, pair, (((1,), (1,)), ((), ())), preferred_element_type=f32)
        return value

    local = lax.fori_loop(0, BLOCKS // 2 // UNROLL, gram_step, jnp.zeros((64, 64), f32))
    local = jnp.concatenate([local, jnp.zeros((64, 64), f32)], axis=1)
    for b in range(8):
        gram[b] = local[8 * b : 8 * b + 8]
    scatter = exchange(lambda peer: gram.at[peer], gram_part, gy, n_gy, on_gy, gram_send, gram_recv, 0)
    gram_part[gy] = gram[gy]

    wait(loads)
    flat_state = flat(state)
    for side in range(2):
        for f in range(5):
            for far in range(2):
                y = Y - 1 - far if side == 0 else far
                for t in range(2):
                    y_out[side, f, far, t] = flat_state[sheet(f, t, 8 + y), :]
    y_copies = [
        remote(y_out.at[side], y_in.at[side], y_send.at[side], y_recv.at[side], moved(0, 1 - 2 * side))
        for side in range(2)
    ]
    start(y_copies)
    corner_out[...] = jnp.zeros_like(corner_out)
    corner_copies = []
    for side_x in range(2):
        for side_y in range(2):
            x, y = (X - 1) * (1 - side_x), (Y - 1) * (1 - side_y)
            for t in range(2):
                begin = ((2 + x) * 2 + t) * YP + 8 + y
                corner_out[side_x, side_y, t, 0:5] = flat_state[pl.ds(begin, 5, stride=XP * STEP_X), :]
            at = side_x * 2 + side_y
            corner_copies.append(
                remote(
                    corner_out.at[side_x, side_y], corner_in.at[side_x, side_y],
                    corner_send.at[at], corner_recv.at[at], moved(1 - 2 * side_x, 1 - 2 * side_y),
                )
            )
    start(corner_copies)
    start_far(0)

    loop(2, 2 + X, lambda x: primitive_layer(state, prim, x))
    wait(scatter)
    copies = gram_stage(0, total(gram_part, n_gy))
    start_far(1)
    wait(y_copies)
    for side in range(2):
        place_rows(state, prim, y_in, side)
    loop(3, 1 + X, lambda x: first_layer(state, prim, state2, prim2, x))
    sums[...] = jnp.zeros_like(sums)
    wait(copies)
    copies = gram_stage(1, total(second[0], second[2]))
    start_far(2)
    wait(near_copies + corner_copies)
    loop(0, 2, lambda i: primitive_layer(state, prim, 1 + 9 * i))
    for side_x in range(2):
        for side_y in range(2):
            place_corner(state, prim, corner_in, side_x, side_y)
    loop(0, 2, lambda i: first_layer(state, prim, state2, prim2, 2 + 7 * i))
    for side in range(2):
        edge_rows(state, prim, state2, prim2, y_in, side)
    wait(copies)
    gram_sums[2] = total(third[0], third[2])
    gather = exchange(lambda peer: gram_sums.at[2], gram_all, gy, n_gy, on_gy, gram_send, gram_recv, 24)
    gram_all[gy] = gram_sums[2]
    loop(3, 1 + X, lambda x: second_layer(state, state2, prim2, updated, sums, x))
    lane = lax.broadcasted_iota(jnp.int32, (8, 128), 1)
    sub = lax.broadcasted_iota(jnp.int32, (8, 128), 0)

    def factor_start():
        wait(gather)
        blocks = []
        for b in range(8):
            row = sub + 8 * b
            known = (row < SNAPS) & (lane < SNAPS)
            unit = ((lane == row) & (row == SNAPS)) | (lane == row + 64)
            blocks.append(jnp.where(known, gram_all[b] / rows_all, jnp.where(unit, 1.0, 0.0)))
        return eliminate(blocks, 0, SPLIT)

    if FACTOR_AT == 2:
        blocks = factor_start()
    for half in range(2):
        wait(far_copies[half])
        begin, end = CHUNK * half, CHUNK * half + CHUNK
        for i in range(2):
            primitive_layer(state, prim, 11 * i, begin, end)
        for i in range(2):
            first_layer(state, prim, state2, prim2, 1 + 9 * i, begin, end)
        for i in range(2):
            second_layer(state, state2, prim2, updated, sums, 2 + 7 * i, begin, end)

    flat_sums = flat(sums)
    columns = []
    for half in range(2):
        for t in range(2):
            parts = []
            for c in range(6):
                begin = (c * 2 + t) * Y + 4 * half
                part = flat_sums[pl.ds(begin, 8, stride=8), :]
                for k in range(1, 4):
                    part = part + flat_sums[pl.ds(begin + k, 8, stride=8), :]
                parts.append(part)
            columns.append(jnp.concatenate(parts, axis=0))
    fine = jnp.concatenate(columns, axis=1)
    source = lax.broadcasted_iota(jnp.int32, (512, 128), 0)
    target = lax.broadcasted_iota(jnp.int32, (512, 128), 1)
    selection = jnp.where(lax.shift_right_logical(source, 2) == target, 1.0 / 64.0, 0.0).astype(bf16)
    means = sum(jnp.dot(part, selection, preferred_element_type=f32) for part in split3(fine))
    for c in range(3):
        for half in range(2):
            at = (2 * c + half) * 8
            coarse[pl.ds(16 * c + half, 8, stride=2), :] = means[at : at + 8]

    partial = [jnp.zeros((64, 128), f32) for _ in range(2)]
    for b in range(BLOCKS):
        partial[b % 2] = partial[b % 2] + flat_snap[pl.ds(b, 64, stride=BLOCKS), :] * coarse[pl.ds(b, 1), :]
    acc = partial[0] + partial[1]
    squares = jnp.sum(coarse[...] * coarse[...], axis=0, keepdims=True)
    acc = jnp.where(lax.broadcasted_iota(jnp.int32, (64, 128), 0) == SNAPS, squares, acc)
    ones = jnp.ones((8, 128), bf16)
    products = sum(
        lax.dot_general(ones, part, (((1,), (1,)), ((), ())), preferred_element_type=f32) for part in split3(acc)
    )
    dot_sums[0] = jnp.concatenate([products, jnp.zeros((8, 64), f32)], axis=1)
    copies = exchange(lambda peer: dot_sums.at[0], dot_gy, gy, n_gy, on_gy, dot_send, dot_recv, 0)
    dot_gy[gy] = dot_sums[0]

    stores = []
    for t in range(2):
        lanes = pl.ds(128 * t, 128)
        stores += [
            pltpu.make_async_copy(updated.at[0, :, t], out_density.at[:, :, lanes], store_sem.at[3 * t]),
            pltpu.make_async_copy(updated.at[pl.ds(1, 3), :, t], out_momentum.at[:, :, :, lanes], store_sem.at[3 * t + 1]),
            pltpu.make_async_copy(updated.at[4, :, t], out_energy.at[:, :, lanes], store_sem.at[3 * t + 2]),
        ]
    start(stores)
    if FACTOR_AT == 0:
        blocks = factor_start()
    wait(copies)
    dot_sums[1] = total(dot_gy, n_gy)
    copies = exchange(lambda peer: dot_sums.at[1], dot_z, iz, n_z, on_z, dot_send, dot_recv, 8)
    dot_z[iz] = dot_sums[1]
    if FACTOR_AT == 1:
        blocks = factor_start()
    blocks = eliminate(blocks, SPLIT, 8)
    for b in range(8):
        row = sub + 8 * b
        diagonal = jnp.sum(jnp.where(lane == row, blocks[b], 0.0), axis=1, keepdims=True)
        scaled = blocks[b] * (1.0 / jnp.sqrt(diagonal))
        factor_v[b] = jnp.where((lane >= row) & (lane < SNAPS), scaled, 0.0)
        lower_v[b] = jnp.where((row < SNAPS) & (lane < 64), pltpu.roll(scaled, 64, 1), 0.0)
    wait(copies)
    dot_sums[2] = total(dot_z, n_z)
    copies = exchange(lambda peer: dot_sums.at[2], dot_y, iy, n_y, on_y, dot_send, dot_recv, 16)
    dot_y[iy] = dot_sums[2]
    stacked = jnp.concatenate(split3(lower_v[...].reshape(64, 128)[:, :64]), axis=0)

    def modes_step(i, carry):
        for part in range(BLOCKS // 2):
            at = BLOCKS // 2 * i + part
            parts = jnp.dot(stacked, snap_b[at], preferred_element_type=f32)
            both = parts[0:64] + (parts[64:128] + parts[128:192])
            for half in range(2):
                flat_modes[pl.ds(2 * at + half, 64, stride=BLOCKS), :] = both[:, 128 * half : 128 * half + 128]
        return carry

    lax.fori_loop(0, 1, modes_step, 0)
    store_modes = pltpu.make_async_copy(
        flat_modes.at[pl.ds(0, SNAPS * BLOCKS)], out_modes, store_sem.at[6]
    )
    store_modes.start()
    wait(copies)
    share = total(dot_y, n_y) / rows_all

    own = jnp.where(lane < SNAPS, share, 0.0)
    weights = [jnp.sum(lower_v[b] * own, axis=1, keepdims=True) for b in range(8)]
    norm = jnp.sum(jnp.where(lane == SNAPS, share, 0.0), axis=1, keepdims=True)[0:1]
    norm = norm - jnp.sum(sum(weight * weight for weight in weights), axis=0, keepdims=True)
    last = jnp.broadcast_to(jnp.sqrt(norm), (8, 128))
    mode = [[coarse[8 * i : 8 * i + 8, :], jnp.zeros((8, 128), f32)] for i in range(6)]
    for b in range(8):
        row = sub + 8 * b
        weight = jnp.broadcast_to(weights[b], (8, 128))
        column = jnp.where(row == SNAPS, last, weight)
        out_factor[8 * b : 8 * b + 8, :] = jnp.where(lane == SNAPS, column, factor_v[b])[:, :64]
        for at in range(8 if b < 7 else 7):
            one = jnp.broadcast_to(weight[at : at + 1], (8, 128))
            begin = BLOCKS * (8 * b + at)
            for i in range(6):
                mode[i][at % 2] = mode[i][at % 2] - one * flat_modes[begin + 8 * i : begin + 8 * i + 8, :]
    scale = 1.0 / last
    for i in range(6):
        out_last[8 * i : 8 * i + 8, :] = (mode[i][0] + mode[i][1]) * scale
    wait(stores + [store_modes])


def copy_out(*refs):
    sources, targets, sem = refs[:6], refs[6:11], refs[11]
    copies = []

    def add(source, target):
        copies.append(pltpu.make_async_copy(source, target, sem.at[len(copies)]))

    add(sources[4], targets[4].at[pl.ds(0, SNAPS * BLOCKS)])
    add(sources[0], targets[0])
    for c in range(3):
        add(sources[1].at[c], targets[1].at[c])
    add(sources[2], targets[2])
    add(sources[5], targets[4].at[pl.ds(SNAPS * BLOCKS, BLOCKS)])
    add(sources[3], targets[3])
    for copy in copies:
        copy.start()
    for copy in copies:
        copy.wait()


def solution(mesh):
    n_gx, n_gy = mesh.shape["gx"], mesh.shape["gy"]
    n_y = 4
    n_z = n_gx // n_y

    def on_device(density, momentum, energy, snapshots):
        rows_all = 6144 * n_gx * n_gy
        snapshots = snapshots.reshape(SNAPS, 3, 2, 8, 128).transpose(0, 1, 3, 2, 4).reshape(SNAPS, 3, 16, 128)
        anywhere = pl.BlockSpec(memory_space=pl.ANY)
        vmem = pl.BlockSpec(memory_space=pltpu.VMEM)
        dma = pltpu.SemaphoreType.DMA
        results = pl.pallas_call(
            functools.partial(kernel, float(rows_all), (n_gx, n_gy, n_y)),
            name="sections_and_modes",
            in_specs=[pl.BlockSpec(memory_space=pltpu.HBM)] * 4,
            out_specs=(anywhere, anywhere, anywhere, vmem, anywhere, vmem),
            out_shape=(
                jax.ShapeDtypeStruct((X, Y, Z), f32),
                jax.ShapeDtypeStruct((3, X, Y, Z), f32),
                jax.ShapeDtypeStruct((X, Y, Z), f32),
                jax.ShapeDtypeStruct((64, 64), f32),
                jax.ShapeDtypeStruct((SNAPS * BLOCKS, 128), f32),
                jax.ShapeDtypeStruct((BLOCKS, 128), f32),
            ),
            scratch_shapes=[
                pltpu.VMEM((5, XP, 2, YP, 128), f32),
                pltpu.VMEM((4, XP, 2, YP, 128), f32),
                pltpu.VMEM((5, XP, 2, YP, 128), f32),
                pltpu.VMEM((4, XP, 2, YP, 128), f32),
                pltpu.VMEM((5, X, 2, Y, 128), f32),
                pltpu.VMEM((3, 2, 2, Y, 128), f32),
                pltpu.VMEM((2, 5, 2, 2, 8, 128), f32),
                pltpu.VMEM((2, 5, 2, 2, 8, 128), f32),
                pltpu.VMEM((2, 2, 2, 8, 128), f32),
                pltpu.VMEM((2, 2, 2, 8, 128), f32),
                pltpu.VMEM((SNAPS, 3, 16, 128), bf16),
                pltpu.VMEM((64, 3, 16, 128), f32),
                pltpu.VMEM((BLOCKS // 2, 64, 256), bf16),
                pltpu.VMEM((64, 3, 16, 128), f32),
                pltpu.VMEM((8, 8, 128), f32),
                pltpu.VMEM((8, 8, 128), f32),
                pltpu.VMEM((BLOCKS, 128), f32),
                pltpu.VMEM((8, 8, 128), f32),
                pltpu.VMEM((n_gy, 8, 128), f32),
                pltpu.VMEM((n_z, 8, 128), f32),
                pltpu.VMEM((n_y, 8, 128), f32),
                pltpu.VMEM((8, 8, 128), f32),
                pltpu.VMEM((3, 8, 128), f32),
                pltpu.VMEM((n_gy, 8, 128), f32),
                pltpu.VMEM((n_z, 8, 128), f32),
                pltpu.VMEM((n_y, 8, 128), f32),
                pltpu.VMEM((4, 8, 128), f32),
                dma((7,)),
                dma((7,)),
                dma((36,)),
                dma((36,)),
                dma((2,)),
                dma((2,)),
                dma((4,)),
                dma((4,)),
                dma((32,)),
                dma((32,)),
                dma((24,)),
                dma((24,)),
            ],
            compiler_params=pltpu.CompilerParams(
                collective_id=0, has_side_effects=True, vmem_limit_bytes=32 * 2**20
            ),
        )(*(pltpu.with_memory_space_constraint(a, pltpu.HBM) for a in (density, momentum, energy, snapshots)))
        new_density, new_momentum, new_energy, factor, modes = pl.pallas_call(
            copy_out,
            name="copy_out",
            in_specs=[anywhere] * 6,
            out_specs=[pl.BlockSpec(memory_space=pltpu.HBM)] * 5,
            out_shape=[jax.ShapeDtypeStruct(value.shape, f32) for value in results[:4]]
            + [jax.ShapeDtypeStruct((64 * BLOCKS, 128), f32)],
            scratch_shapes=[dma((8,))],
            compiler_params=pltpu.CompilerParams(vmem_limit_bytes=2**20),
        )(*results)
        modes = modes.reshape(64, 3, 8, 2, 128).transpose(0, 1, 3, 2, 4).reshape(64, 3, 2, 1024)
        return new_density, new_momentum, new_energy, factor, modes

    placed = (
        P("gx", "gy", None),
        P(None, "gx", "gy", None),
        P("gx", "gy", None),
        P(None, None, "gx", "gy"),
    )
    return jax.shard_map(
        on_device,
        mesh=mesh,
        in_specs=placed,
        out_specs=(
            P("gx", "gy", None),
            P(None, "gx", "gy", None),
            P("gx", "gy", None),
            P(),
            P(None, None, "gx", "gy"),
        ),
        check_vma=False,
    )
```

```python
import functools

import jax
import jax.numpy as jnp
from jax import lax
from jax.experimental import pallas as pl
from jax.experimental.pallas import tpu as pltpu
from jax.sharding import PartitionSpec as P

f32 = jnp.float32
bf16 = jnp.bfloat16
MESH = pl.DeviceIdType.MESH

time_step = 0.08
shear_friction_coefficient = 1.5
heat_conduction_coefficient = 1.5

X, Y, Z = 8, 64, 256
XP, YP = 12, 80
STEP_X = 2 * YP
SNAPS = 63
BLOCKS = 48
CHUNK = 32
UNROLL = 8
FAR_LOW = 1
FAR_HIGH = 2
Y_FIRST = True
FACTOR_AT = 1
SPLIT = 4


def flat(ref):
    rows = 1
    for size in ref.shape[:-1]:
        rows *= size
    return ref.reshape(rows, 128)


def split3(value):
    high = value.astype(bf16)
    rest = value - high.astype(f32)
    middle = rest.astype(bf16)
    low = (rest - middle.astype(f32)).astype(bf16)
    return high, middle, low


def z_pair(pair, copied):
    low, high = pair
    lane = lax.broadcasted_iota(jnp.int32, low.shape, 1)
    last, first = lane == 127, lane == 0
    low_up, high_up = pltpu.roll(low, 127, 1), pltpu.roll(high, 127, 1)
    low_down, high_down = pltpu.roll(low, 1, 1), pltpu.roll(high, 1, 1)
    above, below = (high, low) if copied else (0.0, 0.0)
    up = (jnp.where(last, high_up, low_up), jnp.where(last, above, high_up))
    down = (jnp.where(first, below, low_down), jnp.where(first, low_down, high_down))
    return up, down


def primitives(state):
    inverse = 1.0 / state[0]
    return [state[1 + field] * inverse for field in range(4)]


def change(center, x_up, x_down, y_up, y_down, mx_up, mx_down, my_up, my_down, mz):
    up, down = z_pair(mz, False)
    result = [
        [
            (-0.5 * time_step) * ((mx_up[t] - mx_down[t]) + (my_up[t] - my_down[t]) + (up[t] - down[t]))
            for t in range(2)
        ]
    ]
    for field in range(4):
        rate = heat_conduction_coefficient if field == 3 else shear_friction_coefficient
        up, down = z_pair(center[field], field == 3)
        result.append(
            [
                (time_step * rate)
                * (
                    (x_up[field][t] + x_down[field][t])
                    + (y_up[field][t] + y_down[field][t])
                    + (up[t] + down[t])
                    - 6.0 * center[field][t]
                )
                for t in range(2)
            ]
        )
    return result


def change_rows(prim, state, x, row, count):
    def v(dx, dy):
        return [[prim[f, x + dx, t, pl.ds(row + dy, count), :] for t in range(2)] for f in range(4)]

    def s(field, dx, dy):
        return [state[field, x + dx, t, pl.ds(row + dy, count), :] for t in range(2)]

    return change(
        v(0, 0), v(1, 0), v(-1, 0), v(0, 1), v(0, -1),
        s(1, 1, 0), s(1, -1, 0), s(2, 0, 1), s(2, 0, -1), s(3, 0, 0),
    )


def primitive_layer(state, prim, x, begin=0, end=Y):
    for row in range(8 + begin, 8 + end, CHUNK):
        for t in range(2):
            values = primitives([state[f, x, t, pl.ds(row, CHUNK), :] for f in range(5)])
            for f in range(4):
                prim[f, x, t, pl.ds(row, CHUNK), :] = values[f]


def first_layer(state, prim, state2, prim2, x, begin=0, end=Y):
    for row in range(8 + begin, 8 + end, CHUNK):
        delta = change_rows(prim, state, x, row, CHUNK)
        for t in range(2):
            new = [state[f, x, t, pl.ds(row, CHUNK), :] + delta[f][t] for f in range(5)]
            values = primitives(new)
            for f in range(5):
                state2[f, x, t, pl.ds(row, CHUNK), :] = new[f]
            for f in range(4):
                prim2[f, x, t, pl.ds(row, CHUNK), :] = values[f]


def second_layer(state, state2, prim2, updated, sums, x, begin=0, end=Y):
    for row in range(8 + begin, 8 + end, CHUNK):
        delta = change_rows(prim2, state2, x, row, CHUNK)
        for t in range(2):
            new = [
                0.5 * state[f, x, t, pl.ds(row, CHUNK), :]
                + 0.5 * (state2[f, x, t, pl.ds(row, CHUNK), :] + delta[f][t])
                for f in range(5)
            ]
            inverse = 1.0 / new[0]
            for f in range(5):
                updated[f, x - 2, t, pl.ds(row - 8, CHUNK), :] = new[f]
            for c in range(3):
                sums[c, (x - 2) // 4, t, pl.ds(row - 8, CHUNK), :] += new[1 + c] * inverse


def sheet(field, tile, row, dx=0):
    return pl.ds(((field * XP + 2 + dx) * 2 + tile) * YP + row, X, stride=STEP_X)


def place_rows(state, prim, y_in, side):
    row = 7 if side == 0 else 72
    flat_state, flat_prim = flat(state), flat(prim)
    for t in range(2):
        near = [y_in[side, f, 0, t] for f in range(5)]
        values = primitives(near)
        for f in range(4):
            flat_prim[sheet(f, t, row), :] = values[f]
        for f in (1, 2):
            flat_state[sheet(f, t, row), :] = near[f]


def place_corner(state, prim, corner_in, side_x, side_y):
    x = 1 if side_x == 0 else 10
    row = 7 if side_y == 0 else 72
    for t in range(2):
        values = corner_in[side_x, side_y, t]
        inverse = 1.0 / values[0:1]
        for f in range(4):
            prim[f, x, t, pl.ds(row, 1), :] = values[1 + f : 2 + f] * inverse
        for f in (1, 2):
            state[f, x, t, pl.ds(row, 1), :] = values[f : f + 1]


def edge_rows(state, prim, state2, prim2, y_in, side):
    row, own = (7, 8) if side == 0 else (72, 71)
    flat_state, flat_prim = flat(state), flat(prim)
    flat_state2, flat_prim2 = flat(state2), flat(prim2)

    def v(at, dx):
        return [[flat_prim[sheet(f, t, at, dx), :] for t in range(2)] for f in range(4)]

    def s(field, at, dx):
        return [flat_state[sheet(field, t, at, dx), :] for t in range(2)]

    near = [[y_in[side, f, 0, t] for f in range(5)] for t in range(2)]
    far = [primitives([y_in[side, f, 1, t] for f in range(5)]) for t in range(2)]
    far = [[far[t][f] for t in range(2)] for f in range(4)]
    far_my = [y_in[side, 2, 1, t] for t in range(2)]
    inner, inner_my = v(own, 0), s(2, own, 0)
    y_up, y_down, my_up, my_down = (
        (inner, far, inner_my, far_my) if side == 0 else (far, inner, far_my, inner_my)
    )
    delta = change(
        v(row, 0), v(row, 1), v(row, -1), y_up, y_down,
        s(1, row, 1), s(1, row, -1), my_up, my_down, [near[t][3] for t in range(2)],
    )
    for t in range(2):
        new = [near[t][f] + delta[f][t] for f in range(5)]
        values = primitives(new)
        for f in range(4):
            flat_prim2[sheet(f, t, row), :] = values[f]
        flat_state2[sheet(2, t, row), :] = new[2]


def eliminate(rows, first, stop):
    sub = lax.broadcasted_iota(jnp.int32, (8, 128), 0)
    for block in range(first, stop):
        columns = [
            [jnp.broadcast_to(rows[b][:, 8 * block + j : 8 * block + j + 1], (8, 128)) for b in range(block, 8)]
            for j in range(8)
        ]
        corner = {
            (i, j): jnp.broadcast_to(columns[j][0][i : i + 1, :], (8, 128)) for j in range(8) for i in range(j, 8)
        }
        pivot_rows = [jnp.broadcast_to(rows[block][i : i + 1, :], (8, 128)) for i in range(8)]
        for j in range(8):
            inverse = 1.0 / corner[j, j]
            ratio = {i: corner[i, j] * inverse for i in range(j + 1, 8)}
            for i in range(j + 1, 8):
                for n in range(j + 1, i + 1):
                    corner[i, n] = corner[i, n] - ratio[i] * corner[n, j]
                pivot_rows[i] = pivot_rows[i] - ratio[i] * pivot_rows[j]
                for b in range(8 - block):
                    columns[i][b] = columns[i][b] - ratio[i] * columns[j][b]
            scaled = pivot_rows[j] * inverse
            for b in range(8 - block):
                column = jnp.where(sub > j, columns[j][b], 0.0) if b == 0 else columns[j][b]
                rows[block + b] = rows[block + b] - column * scaled
    return rows


def kernel(
    rows_all, sizes,
    density, momentum, energy, snapshots,
    out_density, out_momentum, out_energy, out_factor, out_modes, out_last,
    state, prim, state2, prim2, updated, sums,
    y_out, y_in, corner_out, corner_in,
    snap_in, snap_f, snap_b, modes, factor_v, lower_v, coarse,
    gram, gram_part, gram_z, gram_y, gram_all, gram_sums,
    dot_gy, dot_z, dot_y, dot_sums,
    load_sem, store_sem,
    x_send, x_recv, y_send, y_recv, corner_send, corner_recv,
    gram_send, gram_recv, dot_send, dot_recv,
):
    n_gx, n_gy, n_y = sizes
    n_z = n_gx // n_y
    gx, gy = lax.axis_index("gx"), lax.axis_index("gy")
    iz, iy = lax.div(gx, n_y), lax.rem(gx, n_y)

    def moved(dx, dy):
        return {"gx": lax.rem(gx + dx + n_gx, n_gx), "gy": lax.rem(gy + dy + n_gy, n_gy)}

    def on_gy(i):
        return {"gx": gx, "gy": i}

    def on_z(i):
        return {"gx": i * n_y + iy, "gy": gy}

    def on_y(i):
        return {"gx": iz * n_y + i, "gy": gy}

    loads = []
    for t in range(2):
        lanes, rows = pl.ds(128 * t, 128), pl.ds(8, Y)
        loads += [
            pltpu.make_async_copy(density.at[:, :, lanes], state.at[0, pl.ds(2, X), t, rows, :], load_sem.at[3 * t]),
            pltpu.make_async_copy(
                momentum.at[:, :, :, lanes], state.at[pl.ds(1, 3), pl.ds(2, X), t, rows, :], load_sem.at[3 * t + 1]
            ),
            pltpu.make_async_copy(energy.at[:, :, lanes], state.at[4, pl.ds(2, X), t, rows, :], load_sem.at[3 * t + 2]),
        ]
    load_snapshots = pltpu.make_async_copy(snapshots, snap_in, load_sem.at[6])
    for copy in loads:
        copy.start()
    load_snapshots.start()

    barrier = pltpu.get_barrier_semaphore()
    greeted = [moved(dx, dy) for dx in (-1, 1) for dy in (-1, 0, 1)]
    greeted += [on_gy(lax.rem(gy + d, n_gy)) for d in range(1, n_gy)]
    greeted += [on_z(lax.rem(iz + d, n_z)) for d in range(1, n_z)]
    greeted += [on_y(lax.rem(iy + d, n_y)) for d in range(1, n_y)]
    for device in greeted:
        pl.semaphore_signal(barrier, inc=1, device_id=device, device_id_type=MESH)
    pl.semaphore_wait(barrier, len(greeted))

    def remote(source, target, send_sem, recv_sem, device):
        return pltpu.make_async_remote_copy(
            src_ref=source, dst_ref=target, send_sem=send_sem, recv_sem=recv_sem, device_id=device, device_id_type=MESH
        )

    def x_copies(layer, begin, count, at):
        copies = []
        for side in range(2):
            source, target = (X - 1 - layer, 1 - layer) if side == 0 else (layer, 10 + layer)
            device = moved(1, 0) if side == 0 else moved(-1, 0)
            own, rows = pl.ds(begin, count), pl.ds(8 + begin, count)
            for t in range(2):
                lanes = pl.ds(128 * t, 128)
                copies += [
                    remote(
                        density.at[source, own, lanes], state.at[0, target, t, rows, :],
                        x_send.at[at], x_recv.at[at], device,
                    ),
                    remote(
                        momentum.at[:, source, own, lanes], state.at[pl.ds(1, 3), target, t, rows, :],
                        x_send.at[at + 1], x_recv.at[at + 1], device,
                    ),
                    remote(
                        energy.at[source, own, lanes], state.at[4, target, t, rows, :],
                        x_send.at[at + 2], x_recv.at[at + 2], device,
                    ),
                ]
                at += 3
        return copies

    def start(copies):
        for copy in copies:
            copy.start()

    def wait(copies):
        for copy in copies:
            copy.wait()

    def loop(first, stop, step):
        lax.fori_loop(first, stop, lambda x, _: (step(x), 0)[1], 0)

    def exchange(sources, target, me, count, device_of, send, recv, first):
        copies = []
        for d in sorted(range(1, count), key=lambda d: -min(d, count - d)):
            peer = lax.rem(me + d, count)
            copies.append(
                remote(sources(peer), target.at[me], send.at[first + d], recv.at[first + d], device_of(peer))
            )
        start(copies)
        return copies

    def total(ref, count):
        value = ref[0]
        for i in range(1, count):
            value = value + ref[i]
        return value

    near_copies = x_copies(0, 0, Y, 0)
    far_copies = [x_copies(1, CHUNK * half, CHUNK, 12 + 12 * half) for half in range(2)]

    def start_far(point):
        for half, chosen in enumerate((FAR_LOW, FAR_HIGH)):
            if chosen == point:
                start(far_copies[half])

    along_z, along_y = (gram_z, iz, n_z, on_z), (gram_y, iy, n_y, on_y)
    second, third = (along_y, along_z) if Y_FIRST else (along_z, along_y)

    def gram_stage(stage, value):
        target, me, count, device_of = (second, third)[stage]
        gram_sums[stage] = value
        copies = exchange(lambda peer: gram_sums.at[stage], target, me, count, device_of, gram_send, gram_recv, 8 + 8 * stage)
        target[me] = value
        return copies

    start(near_copies)

    load_snapshots.wait()
    for c in range(3):
        snap_f[0:SNAPS, c] = snap_in[:, c].astype(f32)
    snap_f[SNAPS] = jnp.zeros((3, 16, 128), f32)
    flat_snap, flat_modes = flat(snap_f), flat(modes)

    def gram_step(i, value):
        for part in range(UNROLL):
            at = UNROLL * i + part
            pair = [flat_snap[pl.ds(2 * at + half, 64, stride=BLOCKS), :] for half in range(2)]
            pair = jnp.concatenate(pair, axis=1).astype(bf16)
            snap_b[at] = pair
            value = value + lax.dot_general(pair, pair, (((1,), (1,)), ((), ())), preferred_element_type=f32)
        return value

    local = lax.fori_loop(0, BLOCKS // 2 // UNROLL, gram_step, jnp.zeros((64, 64), f32))
    local = jnp.concatenate([local, jnp.zeros((64, 64), f32)], axis=1)
    for b in range(8):
        gram[b] = local[8 * b : 8 * b + 8]
    scatter = exchange(lambda peer: gram.at[peer], gram_part, gy, n_gy, on_gy, gram_send, gram_recv, 0)
    gram_part[gy] = gram[gy]

    wait(loads)
    flat_state = flat(state)
    for side in range(2):
        for f in range(5):
            for far in range(2):
                y = Y - 1 - far if side == 0 else far
                for t in range(2):
                    y_out[side, f, far, t] = flat_state[sheet(f, t, 8 + y), :]
    y_copies = [
        remote(y_out.at[side], y_in.at[side], y_send.at[side], y_recv.at[side], moved(0, 1 - 2 * side))
        for side in range(2)
    ]
    start(y_copies)
    corner_out[...] = jnp.zeros_like(corner_out)
    corner_copies = []
    for side_x in range(2):
        for side_y in range(2):
            x, y = (X - 1) * (1 - side_x), (Y - 1) * (1 - side_y)
            for t in range(2):
                begin = ((2 + x) * 2 + t) * YP + 8 + y
                corner_out[side_x, side_y, t, 0:5] = flat_state[pl.ds(begin, 5, stride=XP * STEP_X), :]
            at = side_x * 2 + side_y
            corner_copies.append(
                remote(
                    corner_out.at[side_x, side_y], corner_in.at[side_x, side_y],
                    corner_send.at[at], corner_recv.at[at], moved(1 - 2 * side_x, 1 - 2 * side_y),
                )
            )
    start(corner_copies)
    start_far(0)

    loop(2, 2 + X, lambda x: primitive_layer(state, prim, x))
    wait(scatter)
    copies = gram_stage(0, total(gram_part, n_gy))
    start_far(1)
    wait(y_copies)
    for side in range(2):
        place_rows(state, prim, y_in, side)
    loop(3, 1 + X, lambda x: first_layer(state, prim, state2, prim2, x))
    sums[...] = jnp.zeros_like(sums)
    wait(copies)
    copies = gram_stage(1, total(second[0], second[2]))
    start_far(2)
    wait(near_copies + corner_copies)
    loop(0, 2, lambda i: primitive_layer(state, prim, 1 + 9 * i))
    for side_x in range(2):
        for side_y in range(2):
            place_corner(state, prim, corner_in, side_x, side_y)
    loop(0, 2, lambda i: first_layer(state, prim, state2, prim2, 2 + 7 * i))
    for side in range(2):
        edge_rows(state, prim, state2, prim2, y_in, side)
    wait(copies)
    gram_sums[2] = total(third[0], third[2])
    gather = exchange(lambda peer: gram_sums.at[2], gram_all, gy, n_gy, on_gy, gram_send, gram_recv, 24)
    gram_all[gy] = gram_sums[2]
    loop(3, 1 + X, lambda x: second_layer(state, state2, prim2, updated, sums, x))
    lane = lax.broadcasted_iota(jnp.int32, (8, 128), 1)
    sub = lax.broadcasted_iota(jnp.int32, (8, 128), 0)

    def factor_start():
        wait(gather)
        blocks = []
        for b in range(8):
            row = sub + 8 * b
            known = (row < SNAPS) & (lane < SNAPS)
            unit = ((lane == row) & (row == SNAPS)) | (lane == row + 64)
            blocks.append(jnp.where(known, gram_all[b] / rows_all, jnp.where(unit, 1.0, 0.0)))
        return eliminate(blocks, 0, SPLIT)

    if FACTOR_AT == 2:
        blocks = factor_start()
    for half in range(2):
        wait(far_copies[half])
        begin, end = CHUNK * half, CHUNK * half + CHUNK
        for i in range(2):
            primitive_layer(state, prim, 11 * i, begin, end)
        for i in range(2):
            first_layer(state, prim, state2, prim2, 1 + 9 * i, begin, end)
        for i in range(2):
            second_layer(state, state2, prim2, updated, sums, 2 + 7 * i, begin, end)

    flat_sums = flat(sums)
    columns = []
    for half in range(2):
        for t in range(2):
            parts = []
            for c in range(6):
                begin = (c * 2 + t) * Y + 4 * half
                part = flat_sums[pl.ds(begin, 8, stride=8), :]
                for k in range(1, 4):
                    part = part + flat_sums[pl.ds(begin + k, 8, stride=8), :]
                parts.append(part)
            columns.append(jnp.concatenate(parts, axis=0))
    fine = jnp.concatenate(columns, axis=1)
    source = lax.broadcasted_iota(jnp.int32, (512, 128), 0)
    target = lax.broadcasted_iota(jnp.int32, (512, 128), 1)
    selection = jnp.where(lax.shift_right_logical(source, 2) == target, 1.0 / 64.0, 0.0).astype(bf16)
    means = sum(jnp.dot(part, selection, preferred_element_type=f32) for part in split3(fine))
    for c in range(3):
        for half in range(2):
            at = (2 * c + half) * 8
            coarse[pl.ds(16 * c + half, 8, stride=2), :] = means[at : at + 8]

    partial = [jnp.zeros((64, 128), f32) for _ in range(2)]
    for b in range(BLOCKS):
        partial[b % 2] = partial[b % 2] + flat_snap[pl.ds(b, 64, stride=BLOCKS), :] * coarse[pl.ds(b, 1), :]
    acc = partial[0] + partial[1]
    squares = jnp.sum(coarse[...] * coarse[...], axis=0, keepdims=True)
    acc = jnp.where(lax.broadcasted_iota(jnp.int32, (64, 128), 0) == SNAPS, squares, acc)
    ones = jnp.ones((8, 128), bf16)
    products = sum(
        lax.dot_general(ones, part, (((1,), (1,)), ((), ())), preferred_element_type=f32) for part in split3(acc)
    )
    dot_sums[0] = jnp.concatenate([products, jnp.zeros((8, 64), f32)], axis=1)[0:1]
    copies = exchange(lambda peer: dot_sums.at[0], dot_gy, gy, n_gy, on_gy, dot_send, dot_recv, 0)
    dot_gy[gy] = dot_sums[0]

    stores = []
    for t in range(2):
        lanes = pl.ds(128 * t, 128)
        stores += [
            pltpu.make_async_copy(updated.at[0, :, t], out_density.at[:, :, lanes], store_sem.at[3 * t]),
            pltpu.make_async_copy(updated.at[pl.ds(1, 3), :, t], out_momentum.at[:, :, :, lanes], store_sem.at[3 * t + 1]),
            pltpu.make_async_copy(updated.at[4, :, t], out_energy.at[:, :, lanes], store_sem.at[3 * t + 2]),
        ]
    start(stores)
    if FACTOR_AT == 0:
        blocks = factor_start()
    wait(copies)
    dot_sums[1] = total(dot_gy, n_gy)
    copies = exchange(lambda peer: dot_sums.at[1], dot_z, iz, n_z, on_z, dot_send, dot_recv, 8)
    dot_z[iz] = dot_sums[1]
    if FACTOR_AT == 1:
        blocks = factor_start()
    blocks = eliminate(blocks, SPLIT, 8)
    for b in range(8):
        row = sub + 8 * b
        diagonal = jnp.sum(jnp.where(lane == row, blocks[b], 0.0), axis=1, keepdims=True)
        scaled = blocks[b] * (1.0 / jnp.sqrt(diagonal))
        factor_v[b] = jnp.where((lane >= row) & (lane < SNAPS), scaled, 0.0)
        lower_v[b] = jnp.where((row < SNAPS) & (lane < 64), pltpu.roll(scaled, 64, 1), 0.0)
    wait(copies)
    dot_sums[2] = total(dot_z, n_z)
    copies = exchange(lambda peer: dot_sums.at[2], dot_y, iy, n_y, on_y, dot_send, dot_recv, 16)
    dot_y[iy] = dot_sums[2]
    stacked = jnp.concatenate(split3(lower_v[...].reshape(64, 128)[:, :64]), axis=0)

    def modes_step(i, carry):
        for part in range(BLOCKS // 2):
            at = BLOCKS // 2 * i + part
            parts = jnp.dot(stacked, snap_b[at], preferred_element_type=f32)
            both = parts[0:64] + (parts[64:128] + parts[128:192])
            for half in range(2):
                flat_modes[pl.ds(2 * at + half, 64, stride=BLOCKS), :] = both[:, 128 * half : 128 * half + 128]
        return carry

    lax.fori_loop(0, 1, modes_step, 0)
    store_modes = pltpu.make_async_copy(
        flat_modes.at[pl.ds(0, SNAPS * BLOCKS)], out_modes, store_sem.at[6]
    )
    store_modes.start()
    wait(copies)
    share = jnp.broadcast_to(total(dot_y, n_y), (8, 128)) / rows_all

    own = jnp.where(lane < SNAPS, share, 0.0)
    weights = [jnp.sum(lower_v[b] * own, axis=1, keepdims=True) for b in range(8)]
    norm = jnp.sum(jnp.where(lane == SNAPS, share, 0.0), axis=1, keepdims=True)[0:1]
    norm = norm - jnp.sum(sum(weight * weight for weight in weights), axis=0, keepdims=True)
    last = jnp.broadcast_to(jnp.sqrt(norm), (8, 128))
    mode = [[coarse[8 * i : 8 * i + 8, :], jnp.zeros((8, 128), f32)] for i in range(6)]
    for b in range(8):
        row = sub + 8 * b
        weight = jnp.broadcast_to(weights[b], (8, 128))
        column = jnp.where(row == SNAPS, last, weight)
        out_factor[8 * b : 8 * b + 8, :] = jnp.where(lane == SNAPS, column, factor_v[b])[:, :64]
        for at in range(8 if b < 7 else 7):
            one = jnp.broadcast_to(weight[at : at + 1], (8, 128))
            begin = BLOCKS * (8 * b + at)
            for i in range(6):
                mode[i][at % 2] = mode[i][at % 2] - one * flat_modes[begin + 8 * i : begin + 8 * i + 8, :]
    scale = 1.0 / last
    for i in range(6):
        out_last[8 * i : 8 * i + 8, :] = (mode[i][0] + mode[i][1]) * scale
    wait(stores + [store_modes])


def copy_out(*refs):
    sources, targets, sem = refs[:6], refs[6:11], refs[11]
    copies = []

    def add(source, target):
        copies.append(pltpu.make_async_copy(source, target, sem.at[len(copies)]))

    add(sources[4], targets[4].at[pl.ds(0, SNAPS * BLOCKS)])
    add(sources[0], targets[0])
    for c in range(3):
        add(sources[1].at[c], targets[1].at[c])
    add(sources[2], targets[2])
    add(sources[5], targets[4].at[pl.ds(SNAPS * BLOCKS, BLOCKS)])
    add(sources[3], targets[3])
    for copy in copies:
        copy.start()
    for copy in copies:
        copy.wait()


def solution(mesh):
    n_gx, n_gy = mesh.shape["gx"], mesh.shape["gy"]
    n_y = 4
    n_z = n_gx // n_y

    def on_device(density, momentum, energy, snapshots):
        rows_all = 6144 * n_gx * n_gy
        snapshots = snapshots.reshape(SNAPS, 3, 2, 8, 128).transpose(0, 1, 3, 2, 4).reshape(SNAPS, 3, 16, 128)
        anywhere = pl.BlockSpec(memory_space=pl.ANY)
        vmem = pl.BlockSpec(memory_space=pltpu.VMEM)
        dma = pltpu.SemaphoreType.DMA
        results = pl.pallas_call(
            functools.partial(kernel, float(rows_all), (n_gx, n_gy, n_y)),
            name="sections_and_modes",
            in_specs=[pl.BlockSpec(memory_space=pltpu.HBM)] * 4,
            out_specs=(anywhere, anywhere, anywhere, vmem, anywhere, vmem),
            out_shape=(
                jax.ShapeDtypeStruct((X, Y, Z), f32),
                jax.ShapeDtypeStruct((3, X, Y, Z), f32),
                jax.ShapeDtypeStruct((X, Y, Z), f32),
                jax.ShapeDtypeStruct((64, 64), f32),
                jax.ShapeDtypeStruct((SNAPS * BLOCKS, 128), f32),
                jax.ShapeDtypeStruct((BLOCKS, 128), f32),
            ),
            scratch_shapes=[
                pltpu.VMEM((5, XP, 2, YP, 128), f32),
                pltpu.VMEM((4, XP, 2, YP, 128), f32),
                pltpu.VMEM((5, XP, 2, YP, 128), f32),
                pltpu.VMEM((4, XP, 2, YP, 128), f32),
                pltpu.VMEM((5, X, 2, Y, 128), f32),
                pltpu.VMEM((3, 2, 2, Y, 128), f32),
                pltpu.VMEM((2, 5, 2, 2, 8, 128), f32),
                pltpu.VMEM((2, 5, 2, 2, 8, 128), f32),
                pltpu.VMEM((2, 2, 2, 8, 128), f32),
                pltpu.VMEM((2, 2, 2, 8, 128), f32),
                pltpu.VMEM((SNAPS, 3, 16, 128), bf16),
                pltpu.VMEM((64, 3, 16, 128), f32),
                pltpu.VMEM((BLOCKS // 2, 64, 256), bf16),
                pltpu.VMEM((64, 3, 16, 128), f32),
                pltpu.VMEM((8, 8, 128), f32),
                pltpu.VMEM((8, 8, 128), f32),
                pltpu.VMEM((BLOCKS, 128), f32),
                pltpu.VMEM((8, 8, 128), f32),
                pltpu.VMEM((n_gy, 8, 128), f32),
                pltpu.VMEM((n_z, 8, 128), f32),
                pltpu.VMEM((n_y, 8, 128), f32),
                pltpu.VMEM((8, 8, 128), f32),
                pltpu.VMEM((3, 8, 128), f32),
                pltpu.VMEM((n_gy, 1, 128), f32),
                pltpu.VMEM((n_z, 1, 128), f32),
                pltpu.VMEM((n_y, 1, 128), f32),
                pltpu.VMEM((3, 1, 128), f32),
                dma((7,)),
                dma((7,)),
                dma((36,)),
                dma((36,)),
                dma((2,)),
                dma((2,)),
                dma((4,)),
                dma((4,)),
                dma((32,)),
                dma((32,)),
                dma((24,)),
                dma((24,)),
            ],
            compiler_params=pltpu.CompilerParams(
                collective_id=0, has_side_effects=True, vmem_limit_bytes=32 * 2**20
            ),
        )(*(pltpu.with_memory_space_constraint(a, pltpu.HBM) for a in (density, momentum, energy, snapshots)))
        new_density, new_momentum, new_energy, factor, modes = pl.pallas_call(
            copy_out,
            name="copy_out",
            in_specs=[anywhere] * 6,
            out_specs=[pl.BlockSpec(memory_space=pltpu.HBM)] * 5,
            out_shape=[jax.ShapeDtypeStruct(value.shape, f32) for value in results[:4]]
            + [jax.ShapeDtypeStruct((64 * BLOCKS, 128), f32)],
            scratch_shapes=[dma((8,))],
            compiler_params=pltpu.CompilerParams(vmem_limit_bytes=2**20),
        )(*results)
        modes = modes.reshape(64, 3, 8, 2, 128).transpose(0, 1, 3, 2, 4).reshape(64, 3, 2, 1024)
        return new_density, new_momentum, new_energy, factor, modes

    placed = (
        P("gx", "gy", None),
        P(None, "gx", "gy", None),
        P("gx", "gy", None),
        P(None, None, "gx", "gy"),
    )
    return jax.shard_map(
        on_device,
        mesh=mesh,
        in_specs=placed,
        out_specs=(
            P("gx", "gy", None),
            P(None, "gx", "gy", None),
            P("gx", "gy", None),
            P(),
            P(None, None, "gx", "gy"),
        ),
        check_vma=False,
    )
```

```python
import functools

import jax
import jax.numpy as jnp
from jax import lax
from jax.experimental import pallas as pl
from jax.experimental.pallas import tpu as pltpu
from jax.sharding import PartitionSpec as P

f32 = jnp.float32
bf16 = jnp.bfloat16
MESH = pl.DeviceIdType.MESH

time_step = 0.08
shear_friction_coefficient = 1.5
heat_conduction_coefficient = 1.5

X, Y, Z = 8, 64, 256
XP, YP = 12, 80
STEP_X = 2 * YP
SNAPS = 63
BLOCKS = 48
CHUNK = 32
UNROLL = 8
FAR_LOW = 1
FAR_HIGH = 2
Y_FIRST = True
FACTOR_AT = 1
SPLIT = 4


def flat(ref):
    rows = 1
    for size in ref.shape[:-1]:
        rows *= size
    return ref.reshape(rows, 128)


def split3(value):
    high = value.astype(bf16)
    rest = value - high.astype(f32)
    middle = rest.astype(bf16)
    low = (rest - middle.astype(f32)).astype(bf16)
    return high, middle, low


def z_pair(pair, copied):
    low, high = pair
    lane = lax.broadcasted_iota(jnp.int32, low.shape, 1)
    last, first = lane == 127, lane == 0
    low_up, high_up = pltpu.roll(low, 127, 1), pltpu.roll(high, 127, 1)
    low_down, high_down = pltpu.roll(low, 1, 1), pltpu.roll(high, 1, 1)
    above, below = (high, low) if copied else (0.0, 0.0)
    up = (jnp.where(last, high_up, low_up), jnp.where(last, above, high_up))
    down = (jnp.where(first, below, low_down), jnp.where(first, low_down, high_down))
    return up, down


def primitives(state):
    inverse = 1.0 / state[0]
    return [state[1 + field] * inverse for field in range(4)]


def change(center, x_up, x_down, y_up, y_down, mx_up, mx_down, my_up, my_down, mz):
    up, down = z_pair(mz, False)
    result = [
        [
            (-0.5 * time_step) * ((mx_up[t] - mx_down[t]) + (my_up[t] - my_down[t]) + (up[t] - down[t]))
            for t in range(2)
        ]
    ]
    for field in range(4):
        rate = heat_conduction_coefficient if field == 3 else shear_friction_coefficient
        up, down = z_pair(center[field], field == 3)
        result.append(
            [
                (time_step * rate)
                * (
                    (x_up[field][t] + x_down[field][t])
                    + (y_up[field][t] + y_down[field][t])
                    + (up[t] + down[t])
                    - 6.0 * center[field][t]
                )
                for t in range(2)
            ]
        )
    return result


def change_rows(prim, state, x, row, count):
    def v(dx, dy):
        return [[prim[f, x + dx, t, pl.ds(row + dy, count), :] for t in range(2)] for f in range(4)]

    def s(field, dx, dy):
        return [state[field, x + dx, t, pl.ds(row + dy, count), :] for t in range(2)]

    return change(
        v(0, 0), v(1, 0), v(-1, 0), v(0, 1), v(0, -1),
        s(1, 1, 0), s(1, -1, 0), s(2, 0, 1), s(2, 0, -1), s(3, 0, 0),
    )


def primitive_layer(state, prim, x, begin=0, end=Y):
    for row in range(8 + begin, 8 + end, CHUNK):
        for t in range(2):
            values = primitives([state[f, x, t, pl.ds(row, CHUNK), :] for f in range(5)])
            for f in range(4):
                prim[f, x, t, pl.ds(row, CHUNK), :] = values[f]


def first_layer(state, prim, state2, prim2, x, begin=0, end=Y):
    for row in range(8 + begin, 8 + end, CHUNK):
        delta = change_rows(prim, state, x, row, CHUNK)
        for t in range(2):
            new = [state[f, x, t, pl.ds(row, CHUNK), :] + delta[f][t] for f in range(5)]
            values = primitives(new)
            for f in range(5):
                state2[f, x, t, pl.ds(row, CHUNK), :] = new[f]
            for f in range(4):
                prim2[f, x, t, pl.ds(row, CHUNK), :] = values[f]


def second_layer(state, state2, prim2, updated, sums, x, begin=0, end=Y):
    for row in range(8 + begin, 8 + end, CHUNK):
        delta = change_rows(prim2, state2, x, row, CHUNK)
        for t in range(2):
            new = [
                0.5 * state[f, x, t, pl.ds(row, CHUNK), :]
                + 0.5 * (state2[f, x, t, pl.ds(row, CHUNK), :] + delta[f][t])
                for f in range(5)
            ]
            inverse = 1.0 / new[0]
            for f in range(5):
                updated[f, x - 2, t, pl.ds(row - 8, CHUNK), :] = new[f]
            for c in range(3):
                sums[c, (x - 2) // 4, t, pl.ds(row - 8, CHUNK), :] += new[1 + c] * inverse


def sheet(field, tile, row, dx=0):
    return pl.ds(((field * XP + 2 + dx) * 2 + tile) * YP + row, X, stride=STEP_X)


def place_rows(state, prim, y_in, side):
    row = 7 if side == 0 else 72
    flat_state, flat_prim = flat(state), flat(prim)
    for t in range(2):
        near = [y_in[side, f, 0, t] for f in range(5)]
        values = primitives(near)
        for f in range(4):
            flat_prim[sheet(f, t, row), :] = values[f]
        for f in (1, 2):
            flat_state[sheet(f, t, row), :] = near[f]


def place_corner(state, prim, corner_in, side_x, side_y):
    x = 1 if side_x == 0 else 10
    row = 7 if side_y == 0 else 72
    for t in range(2):
        values = corner_in[side_x, side_y, t]
        inverse = 1.0 / values[0:1]
        for f in range(4):
            prim[f, x, t, pl.ds(row, 1), :] = values[1 + f : 2 + f] * inverse
        for f in (1, 2):
            state[f, x, t, pl.ds(row, 1), :] = values[f : f + 1]


def edge_rows(state, prim, state2, prim2, y_in, side):
    row, own = (7, 8) if side == 0 else (72, 71)
    flat_state, flat_prim = flat(state), flat(prim)
    flat_state2, flat_prim2 = flat(state2), flat(prim2)

    def v(at, dx):
        return [[flat_prim[sheet(f, t, at, dx), :] for t in range(2)] for f in range(4)]

    def s(field, at, dx):
        return [flat_state[sheet(field, t, at, dx), :] for t in range(2)]

    near = [[y_in[side, f, 0, t] for f in range(5)] for t in range(2)]
    far = [primitives([y_in[side, f, 1, t] for f in range(5)]) for t in range(2)]
    far = [[far[t][f] for t in range(2)] for f in range(4)]
    far_my = [y_in[side, 2, 1, t] for t in range(2)]
    inner, inner_my = v(own, 0), s(2, own, 0)
    y_up, y_down, my_up, my_down = (
        (inner, far, inner_my, far_my) if side == 0 else (far, inner, far_my, inner_my)
    )
    delta = change(
        v(row, 0), v(row, 1), v(row, -1), y_up, y_down,
        s(1, row, 1), s(1, row, -1), my_up, my_down, [near[t][3] for t in range(2)],
    )
    for t in range(2):
        new = [near[t][f] + delta[f][t] for f in range(5)]
        values = primitives(new)
        for f in range(4):
            flat_prim2[sheet(f, t, row), :] = values[f]
        flat_state2[sheet(2, t, row), :] = new[2]


def eliminate(rows, first, stop):
    sub = lax.broadcasted_iota(jnp.int32, (8, 128), 0)
    for block in range(first, stop):
        columns = [
            [jnp.broadcast_to(rows[b][:, 8 * block + j : 8 * block + j + 1], (8, 128)) for b in range(block, 8)]
            for j in range(8)
        ]
        corner = {
            (i, j): jnp.broadcast_to(columns[j][0][i : i + 1, :], (8, 128)) for j in range(8) for i in range(j, 8)
        }
        pivot_rows = [jnp.broadcast_to(rows[block][i : i + 1, :], (8, 128)) for i in range(8)]
        for j in range(8):
            inverse = 1.0 / corner[j, j]
            ratio = {i: corner[i, j] * inverse for i in range(j + 1, 8)}
            for i in range(j + 1, 8):
                for n in range(j + 1, i + 1):
                    corner[i, n] = corner[i, n] - ratio[i] * corner[n, j]
                pivot_rows[i] = pivot_rows[i] - ratio[i] * pivot_rows[j]
                for b in range(8 - block):
                    columns[i][b] = columns[i][b] - ratio[i] * columns[j][b]
            scaled = pivot_rows[j] * inverse
            for b in range(8 - block):
                column = jnp.where(sub > j, columns[j][b], 0.0) if b == 0 else columns[j][b]
                rows[block + b] = rows[block + b] - column * scaled
    return rows


def kernel(
    rows_all, sizes,
    density, momentum, energy, snapshots,
    out_density, out_momentum, out_energy, out_factor, out_modes, out_last,
    state, prim, state2, prim2, updated, sums,
    y_out, y_in, corner_out, corner_in,
    snap_in, snap_f, snap_b, modes, factor_v, lower_v, coarse,
    gram, gram_part, gram_z, gram_y, gram_all, gram_sums,
    dot_gy, dot_z, dot_y, dot_sums,
    load_sem, store_sem,
    x_send, x_recv, y_send, y_recv, corner_send, corner_recv,
    gram_send, gram_recv, dot_send, dot_recv,
):
    n_gx, n_gy, n_y = sizes
    n_z = n_gx // n_y
    gx, gy = lax.axis_index("gx"), lax.axis_index("gy")
    iz, iy = lax.div(gx, n_y), lax.rem(gx, n_y)

    def moved(dx, dy):
        return {"gx": lax.rem(gx + dx + n_gx, n_gx), "gy": lax.rem(gy + dy + n_gy, n_gy)}

    def on_gy(i):
        return {"gx": gx, "gy": i}

    def on_z(i):
        return {"gx": i * n_y + iy, "gy": gy}

    def on_y(i):
        return {"gx": iz * n_y + i, "gy": gy}

    loads = []
    for t in range(2):
        lanes, rows = pl.ds(128 * t, 128), pl.ds(8, Y)
        loads += [
            pltpu.make_async_copy(density.at[:, :, lanes], state.at[0, pl.ds(2, X), t, rows, :], load_sem.at[3 * t]),
            pltpu.make_async_copy(
                momentum.at[:, :, :, lanes], state.at[pl.ds(1, 3), pl.ds(2, X), t, rows, :], load_sem.at[3 * t + 1]
            ),
            pltpu.make_async_copy(energy.at[:, :, lanes], state.at[4, pl.ds(2, X), t, rows, :], load_sem.at[3 * t + 2]),
        ]
    load_snapshots = pltpu.make_async_copy(snapshots, snap_in, load_sem.at[6])
    for copy in loads:
        copy.start()
    load_snapshots.start()

    barrier = pltpu.get_barrier_semaphore()
    greeted = [moved(dx, dy) for dx in (-1, 1) for dy in (-1, 0, 1)]
    greeted += [on_gy(lax.rem(gy + d, n_gy)) for d in range(1, n_gy)]
    greeted += [on_z(lax.rem(iz + d, n_z)) for d in range(1, n_z)]
    greeted += [on_y(lax.rem(iy + d, n_y)) for d in range(1, n_y)]
    for device in greeted:
        pl.semaphore_signal(barrier, inc=1, device_id=device, device_id_type=MESH)
    pl.semaphore_wait(barrier, len(greeted))

    def remote(source, target, send_sem, recv_sem, device):
        return pltpu.make_async_remote_copy(
            src_ref=source, dst_ref=target, send_sem=send_sem, recv_sem=recv_sem, device_id=device, device_id_type=MESH
        )

    def x_copies(layer, begin, count, at):
        copies = []
        for side in range(2):
            source, target = (X - 1 - layer, 1 - layer) if side == 0 else (layer, 10 + layer)
            device = moved(1, 0) if side == 0 else moved(-1, 0)
            own, rows = pl.ds(begin, count), pl.ds(8 + begin, count)
            for t in range(2):
                lanes = pl.ds(128 * t, 128)
                copies += [
                    remote(
                        density.at[source, own, lanes], state.at[0, target, t, rows, :],
                        x_send.at[at], x_recv.at[at], device,
                    ),
                    remote(
                        momentum.at[:, source, own, lanes], state.at[pl.ds(1, 3), target, t, rows, :],
                        x_send.at[at + 1], x_recv.at[at + 1], device,
                    ),
                    remote(
                        energy.at[source, own, lanes], state.at[4, target, t, rows, :],
                        x_send.at[at + 2], x_recv.at[at + 2], device,
                    ),
                ]
                at += 3
        return copies

    def start(copies):
        for copy in copies:
            copy.start()

    def wait(copies):
        for copy in copies:
            copy.wait()

    def arrive(copies):
        for copy in copies:
            copy.wait_recv()
        return copies

    def loop(first, stop, step):
        lax.fori_loop(first, stop, lambda x, _: (step(x), 0)[1], 0)

    def exchange(sources, target, me, count, device_of, send, recv, first):
        copies = []
        for d in sorted(range(1, count), key=lambda d: -min(d, count - d)):
            peer = lax.rem(me + d, count)
            copies.append(
                remote(sources(peer), target.at[me], send.at[first + d], recv.at[first + d], device_of(peer))
            )
        start(copies)
        return copies

    def total(ref, count):
        value = ref[0]
        for i in range(1, count):
            value = value + ref[i]
        return value

    near_copies = x_copies(0, 0, Y, 0)
    far_copies = [x_copies(1, CHUNK * half, CHUNK, 12 + 12 * half) for half in range(2)]

    def start_far(point):
        for half, chosen in enumerate((FAR_LOW, FAR_HIGH)):
            if chosen == point:
                start(far_copies[half])

    along_z, along_y = (gram_z, iz, n_z, on_z), (gram_y, iy, n_y, on_y)
    second, third = (along_y, along_z) if Y_FIRST else (along_z, along_y)

    def gram_stage(stage, value):
        target, me, count, device_of = (second, third)[stage]
        gram_sums[stage] = value
        copies = exchange(lambda peer: gram_sums.at[stage], target, me, count, device_of, gram_send, gram_recv, 8 + 8 * stage)
        target[me] = value
        return copies

    start(near_copies)

    load_snapshots.wait()
    for c in range(3):
        snap_f[0:SNAPS, c] = snap_in[:, c].astype(f32)
    snap_f[SNAPS] = jnp.zeros((3, 16, 128), f32)
    flat_snap, flat_modes = flat(snap_f), flat(modes)

    def gram_step(i, value):
        for part in range(UNROLL):
            at = UNROLL * i + part
            pair = [flat_snap[pl.ds(2 * at + half, 64, stride=BLOCKS), :] for half in range(2)]
            pair = jnp.concatenate(pair, axis=1).astype(bf16)
            snap_b[at] = pair
            value = value + lax.dot_general(pair, pair, (((1,), (1,)), ((), ())), preferred_element_type=f32)
        return value

    local = lax.fori_loop(0, BLOCKS // 2 // UNROLL, gram_step, jnp.zeros((64, 64), f32))
    local = jnp.concatenate([local, jnp.zeros((64, 64), f32)], axis=1)
    for b in range(8):
        gram[b] = local[8 * b : 8 * b + 8]
    scatter = exchange(lambda peer: gram.at[peer], gram_part, gy, n_gy, on_gy, gram_send, gram_recv, 0)
    gram_part[gy] = gram[gy]

    wait(loads)
    flat_state = flat(state)
    for side in range(2):
        for f in range(5):
            for far in range(2):
                y = Y - 1 - far if side == 0 else far
                for t in range(2):
                    y_out[side, f, far, t] = flat_state[sheet(f, t, 8 + y), :]
    y_copies = [
        remote(y_out.at[side], y_in.at[side], y_send.at[side], y_recv.at[side], moved(0, 1 - 2 * side))
        for side in range(2)
    ]
    start(y_copies)
    corner_out[...] = jnp.zeros_like(corner_out)
    corner_copies = []
    for side_x in range(2):
        for side_y in range(2):
            x, y = (X - 1) * (1 - side_x), (Y - 1) * (1 - side_y)
            for t in range(2):
                begin = ((2 + x) * 2 + t) * YP + 8 + y
                corner_out[side_x, side_y, t, 0:5] = flat_state[pl.ds(begin, 5, stride=XP * STEP_X), :]
            at = side_x * 2 + side_y
            corner_copies.append(
                remote(
                    corner_out.at[side_x, side_y], corner_in.at[side_x, side_y],
                    corner_send.at[at], corner_recv.at[at], moved(1 - 2 * side_x, 1 - 2 * side_y),
                )
            )
    start(corner_copies)
    start_far(0)

    loop(2, 2 + X, lambda x: primitive_layer(state, prim, x))
    wait(scatter)
    copies = gram_stage(0, total(gram_part, n_gy))
    start_far(1)
    wait(y_copies)
    for side in range(2):
        place_rows(state, prim, y_in, side)
    loop(3, 1 + X, lambda x: first_layer(state, prim, state2, prim2, x))
    sums[...] = jnp.zeros_like(sums)
    wait(copies)
    copies = gram_stage(1, total(second[0], second[2]))
    start_far(2)
    wait(near_copies + corner_copies)
    loop(0, 2, lambda i: primitive_layer(state, prim, 1 + 9 * i))
    for side_x in range(2):
        for side_y in range(2):
            place_corner(state, prim, corner_in, side_x, side_y)
    loop(0, 2, lambda i: first_layer(state, prim, state2, prim2, 2 + 7 * i))
    for side in range(2):
        edge_rows(state, prim, state2, prim2, y_in, side)
    wait(copies)
    gram_sums[2] = total(third[0], third[2])
    gather = exchange(lambda peer: gram_sums.at[2], gram_all, gy, n_gy, on_gy, gram_send, gram_recv, 24)
    gram_all[gy] = gram_sums[2]
    loop(3, 1 + X, lambda x: second_layer(state, state2, prim2, updated, sums, x))
    lane = lax.broadcasted_iota(jnp.int32, (8, 128), 1)
    sub = lax.broadcasted_iota(jnp.int32, (8, 128), 0)

    def factor_start():
        wait(gather)
        blocks = []
        for b in range(8):
            row = sub + 8 * b
            known = (row < SNAPS) & (lane < SNAPS)
            unit = ((lane == row) & (row == SNAPS)) | (lane == row + 64)
            blocks.append(jnp.where(known, gram_all[b] / rows_all, jnp.where(unit, 1.0, 0.0)))
        return eliminate(blocks, 0, SPLIT)

    if FACTOR_AT == 2:
        blocks = factor_start()
    for half in range(2):
        wait(far_copies[half])
        begin, end = CHUNK * half, CHUNK * half + CHUNK
        for i in range(2):
            primitive_layer(state, prim, 11 * i, begin, end)
        for i in range(2):
            first_layer(state, prim, state2, prim2, 1 + 9 * i, begin, end)
        for i in range(2):
            second_layer(state, state2, prim2, updated, sums, 2 + 7 * i, begin, end)

    flat_sums = flat(sums)
    columns = []
    for half in range(2):
        for t in range(2):
            parts = []
            for c in range(6):
                begin = (c * 2 + t) * Y + 4 * half
                part = flat_sums[pl.ds(begin, 8, stride=8), :]
                for k in range(1, 4):
                    part = part + flat_sums[pl.ds(begin + k, 8, stride=8), :]
                parts.append(part)
            columns.append(jnp.concatenate(parts, axis=0))
    fine = jnp.concatenate(columns, axis=1)
    source = lax.broadcasted_iota(jnp.int32, (512, 128), 0)
    target = lax.broadcasted_iota(jnp.int32, (512, 128), 1)
    selection = jnp.where(lax.shift_right_logical(source, 2) == target, 1.0 / 64.0, 0.0).astype(bf16)
    means = sum(jnp.dot(part, selection, preferred_element_type=f32) for part in split3(fine))
    for c in range(3):
        for half in range(2):
            at = (2 * c + half) * 8
            coarse[pl.ds(16 * c + half, 8, stride=2), :] = means[at : at + 8]

    partial = [jnp.zeros((64, 128), f32) for _ in range(2)]
    for b in range(BLOCKS):
        partial[b % 2] = partial[b % 2] + flat_snap[pl.ds(b, 64, stride=BLOCKS), :] * coarse[pl.ds(b, 1), :]
    acc = partial[0] + partial[1]
    squares = jnp.sum(coarse[...] * coarse[...], axis=0, keepdims=True)
    acc = jnp.where(lax.broadcasted_iota(jnp.int32, (64, 128), 0) == SNAPS, squares, acc)
    ones = jnp.ones((8, 128), bf16)
    products = sum(
        lax.dot_general(ones, part, (((1,), (1,)), ((), ())), preferred_element_type=f32) for part in split3(acc)
    )
    dot_sums[0] = jnp.concatenate([products, jnp.zeros((8, 64), f32)], axis=1)[0:1]
    copies = exchange(lambda peer: dot_sums.at[0], dot_gy, gy, n_gy, on_gy, dot_send, dot_recv, 0)
    dot_gy[gy] = dot_sums[0]

    stores = []
    for t in range(2):
        lanes = pl.ds(128 * t, 128)
        stores += [
            pltpu.make_async_copy(updated.at[0, :, t], out_density.at[:, :, lanes], store_sem.at[3 * t]),
            pltpu.make_async_copy(updated.at[pl.ds(1, 3), :, t], out_momentum.at[:, :, :, lanes], store_sem.at[3 * t + 1]),
            pltpu.make_async_copy(updated.at[4, :, t], out_energy.at[:, :, lanes], store_sem.at[3 * t + 2]),
        ]
    start(stores)
    if FACTOR_AT == 0:
        blocks = factor_start()
    sent = arrive(copies)
    dot_sums[1] = total(dot_gy, n_gy)
    copies = exchange(lambda peer: dot_sums.at[1], dot_z, iz, n_z, on_z, dot_send, dot_recv, 8)
    dot_z[iz] = dot_sums[1]
    if FACTOR_AT == 1:
        blocks = factor_start()
    blocks = eliminate(blocks, SPLIT, 8)
    for b in range(8):
        row = sub + 8 * b
        diagonal = jnp.sum(jnp.where(lane == row, blocks[b], 0.0), axis=1, keepdims=True)
        scaled = blocks[b] * (1.0 / jnp.sqrt(diagonal))
        factor_v[b] = jnp.where((lane >= row) & (lane < SNAPS), scaled, 0.0)
        lower_v[b] = jnp.where((row < SNAPS) & (lane < 64), pltpu.roll(scaled, 64, 1), 0.0)
    sent += arrive(copies)
    dot_sums[2] = total(dot_z, n_z)
    copies = exchange(lambda peer: dot_sums.at[2], dot_y, iy, n_y, on_y, dot_send, dot_recv, 16)
    dot_y[iy] = dot_sums[2]
    stacked = jnp.concatenate(split3(lower_v[...].reshape(64, 128)[:, :64]), axis=0)

    def modes_step(i, carry):
        for part in range(BLOCKS // 2):
            at = BLOCKS // 2 * i + part
            parts = jnp.dot(stacked, snap_b[at], preferred_element_type=f32)
            both = parts[0:64] + (parts[64:128] + parts[128:192])
            for half in range(2):
                flat_modes[pl.ds(2 * at + half, 64, stride=BLOCKS), :] = both[:, 128 * half : 128 * half + 128]
        return carry

    lax.fori_loop(0, 1, modes_step, 0)
    store_modes = pltpu.make_async_copy(
        flat_modes.at[pl.ds(0, SNAPS * BLOCKS)], out_modes, store_sem.at[6]
    )
    store_modes.start()
    sent += arrive(copies)
    share = jnp.broadcast_to(total(dot_y, n_y), (8, 128)) / rows_all

    own = jnp.where(lane < SNAPS, share, 0.0)
    weights = [jnp.sum(lower_v[b] * own, axis=1, keepdims=True) for b in range(8)]
    norm = jnp.sum(jnp.where(lane == SNAPS, share, 0.0), axis=1, keepdims=True)[0:1]
    norm = norm - jnp.sum(sum(weight * weight for weight in weights), axis=0, keepdims=True)
    last = jnp.broadcast_to(jnp.sqrt(norm), (8, 128))
    mode = [[coarse[8 * i : 8 * i + 8, :], jnp.zeros((8, 128), f32)] for i in range(6)]
    for b in range(8):
        row = sub + 8 * b
        weight = jnp.broadcast_to(weights[b], (8, 128))
        column = jnp.where(row == SNAPS, last, weight)
        out_factor[8 * b : 8 * b + 8, :] = jnp.where(lane == SNAPS, column, factor_v[b])[:, :64]
        for at in range(8 if b < 7 else 7):
            one = jnp.broadcast_to(weight[at : at + 1], (8, 128))
            begin = BLOCKS * (8 * b + at)
            for i in range(6):
                mode[i][at % 2] = mode[i][at % 2] - one * flat_modes[begin + 8 * i : begin + 8 * i + 8, :]
    scale = 1.0 / last
    for i in range(6):
        out_last[8 * i : 8 * i + 8, :] = (mode[i][0] + mode[i][1]) * scale
    wait(stores + [store_modes])
    for copy in sent:
        copy.wait_send()


def copy_out(*refs):
    sources, targets, sem = refs[:6], refs[6:11], refs[11]
    copies = []

    def add(source, target):
        copies.append(pltpu.make_async_copy(source, target, sem.at[len(copies)]))

    add(sources[4], targets[4].at[pl.ds(0, SNAPS * BLOCKS)])
    add(sources[0], targets[0])
    for c in range(3):
        add(sources[1].at[c], targets[1].at[c])
    add(sources[2], targets[2])
    add(sources[5], targets[4].at[pl.ds(SNAPS * BLOCKS, BLOCKS)])
    add(sources[3], targets[3])
    for copy in copies:
        copy.start()
    for copy in copies:
        copy.wait()


def solution(mesh):
    n_gx, n_gy = mesh.shape["gx"], mesh.shape["gy"]
    n_y = 4
    n_z = n_gx // n_y

    def on_device(density, momentum, energy, snapshots):
        rows_all = 6144 * n_gx * n_gy
        snapshots = snapshots.reshape(SNAPS, 3, 2, 8, 128).transpose(0, 1, 3, 2, 4).reshape(SNAPS, 3, 16, 128)
        anywhere = pl.BlockSpec(memory_space=pl.ANY)
        vmem = pl.BlockSpec(memory_space=pltpu.VMEM)
        dma = pltpu.SemaphoreType.DMA
        results = pl.pallas_call(
            functools.partial(kernel, float(rows_all), (n_gx, n_gy, n_y)),
            name="sections_and_modes",
            in_specs=[pl.BlockSpec(memory_space=pltpu.HBM)] * 4,
            out_specs=(anywhere, anywhere, anywhere, vmem, anywhere, vmem),
            out_shape=(
                jax.ShapeDtypeStruct((X, Y, Z), f32),
                jax.ShapeDtypeStruct((3, X, Y, Z), f32),
                jax.ShapeDtypeStruct((X, Y, Z), f32),
                jax.ShapeDtypeStruct((64, 64), f32),
                jax.ShapeDtypeStruct((SNAPS * BLOCKS, 128), f32),
                jax.ShapeDtypeStruct((BLOCKS, 128), f32),
            ),
            scratch_shapes=[
                pltpu.VMEM((5, XP, 2, YP, 128), f32),
                pltpu.VMEM((4, XP, 2, YP, 128), f32),
                pltpu.VMEM((5, XP, 2, YP, 128), f32),
                pltpu.VMEM((4, XP, 2, YP, 128), f32),
                pltpu.VMEM((5, X, 2, Y, 128), f32),
                pltpu.VMEM((3, 2, 2, Y, 128), f32),
                pltpu.VMEM((2, 5, 2, 2, 8, 128), f32),
                pltpu.VMEM((2, 5, 2, 2, 8, 128), f32),
                pltpu.VMEM((2, 2, 2, 8, 128), f32),
                pltpu.VMEM((2, 2, 2, 8, 128), f32),
                pltpu.VMEM((SNAPS, 3, 16, 128), bf16),
                pltpu.VMEM((64, 3, 16, 128), f32),
                pltpu.VMEM((BLOCKS // 2, 64, 256), bf16),
                pltpu.VMEM((64, 3, 16, 128), f32),
                pltpu.VMEM((8, 8, 128), f32),
                pltpu.VMEM((8, 8, 128), f32),
                pltpu.VMEM((BLOCKS, 128), f32),
                pltpu.VMEM((8, 8, 128), f32),
                pltpu.VMEM((n_gy, 8, 128), f32),
                pltpu.VMEM((n_z, 8, 128), f32),
                pltpu.VMEM((n_y, 8, 128), f32),
                pltpu.VMEM((8, 8, 128), f32),
                pltpu.VMEM((3, 8, 128), f32),
                pltpu.VMEM((n_gy, 1, 128), f32),
                pltpu.VMEM((n_z, 1, 128), f32),
                pltpu.VMEM((n_y, 1, 128), f32),
                pltpu.VMEM((3, 1, 128), f32),
                dma((7,)),
                dma((7,)),
                dma((36,)),
                dma((36,)),
                dma((2,)),
                dma((2,)),
                dma((4,)),
                dma((4,)),
                dma((32,)),
                dma((32,)),
                dma((24,)),
                dma((24,)),
            ],
            compiler_params=pltpu.CompilerParams(
                collective_id=0, has_side_effects=True, vmem_limit_bytes=32 * 2**20
            ),
        )(*(pltpu.with_memory_space_constraint(a, pltpu.HBM) for a in (density, momentum, energy, snapshots)))
        new_density, new_momentum, new_energy, factor, modes = pl.pallas_call(
            copy_out,
            name="copy_out",
            in_specs=[anywhere] * 6,
            out_specs=[pl.BlockSpec(memory_space=pltpu.HBM)] * 5,
            out_shape=[jax.ShapeDtypeStruct(value.shape, f32) for value in results[:4]]
            + [jax.ShapeDtypeStruct((64 * BLOCKS, 128), f32)],
            scratch_shapes=[dma((8,))],
            compiler_params=pltpu.CompilerParams(vmem_limit_bytes=2**20),
        )(*results)
        modes = modes.reshape(64, 3, 8, 2, 128).transpose(0, 1, 3, 2, 4).reshape(64, 3, 2, 1024)
        return new_density, new_momentum, new_energy, factor, modes

    placed = (
        P("gx", "gy", None),
        P(None, "gx", "gy", None),
        P("gx", "gy", None),
        P(None, None, "gx", "gy"),
    )
    return jax.shard_map(
        on_device,
        mesh=mesh,
        in_specs=placed,
        out_specs=(
            P("gx", "gy", None),
            P(None, "gx", "gy", None),
            P("gx", "gy", None),
            P(),
            P(None, None, "gx", "gy"),
        ),
        check_vma=False,
    )
```
